32 devices in a mesh: groups: 2 (over y), tx: 16 (over z, x, core).
Axes of the slice: x: 2, y: 2, z: 4, core: 2. Of those that a mesh axis runs over, the one named last changes fastest.
Arguments:
- tile_state: bfloat16 [64, 64, 64, 128], P(('groups', 'tx')), parts along dimension 0, may hold values from -6 to 6
- cotangent: bfloat16 [64, 64, 64, 128], P(('groups', 'tx')), parts along dimension 0, may hold values from -6 to 6
- neighbours: int32 [64, 8], P(('groups', 'tx')), parts along dimension 0, may hold values from -1 to 31, as said below
- land_mask: int32 [64, 4096], P(('groups', 'tx')), parts along dimension 0, may hold values 0 or 1
- kernel: float32 [49, 128], replicated, may hold values from -0.875 to 0.875
- conv_bias: float32 [128], replicated, may hold values from -3 to 3
- norm_gain: float32 [128], replicated, may hold values from 0.25 to 1.75
- norm_bias: float32 [128], replicated, may hold values from -3 to 3
- w_up: bfloat16 [512, 128], replicated, may hold values from -0.5 to 0.5
- up_bias: float32 [512], replicated, may hold values from -3 to 3
- w_down: bfloat16 [512, 128], replicated, may hold values from -0.25 to 0.25
- down_bias: float32 [128], replicated, may hold values from -3 to 3
- layer_scale: float32 [128], replicated, may hold values from 0.3 to 1
Outputs:
- block_out: bfloat16 [64, 64, 64, 128], P(('groups', 'tx')), parts along dimension 0
- grad_state: bfloat16 [64, 64, 64, 128], P(('groups', 'tx')), parts along dimension 0
- grad_up: float32 [1024, 128], P(('groups', 'tx')), parts along dimension 0
- grad_down: float32 [1024, 128], P(('groups', 'tx')), parts along dimension 0
- grad_kernel: float32 [98, 128], P('groups'), parts along dimension 0
- grad_vectors: float32 [10, 128], P('groups'), parts along dimension 0
- grad_up_bias: float32 [1024], P('groups'), parts along dimension 0
The draws below stay inside these ranges and needn't reach their ends.
There are 2 independent parts, one for each index of `groups`. The reference program is written for one: setup_inputs(seed, part) draws one part's arguments, and reference() takes and returns one part's arrays. A program takes and returns all parts, laid end to end along the dimension named above; an argument that names none is the same for every part. Nothing has to cross between parts.
Inputs may be any that keep to these rules, and one draw needn't show every extreme that they name: `neighbours`: each entry is -1 or the slot of another tile whose slot // 2 differs from the tile's own slot // 2 by at most 2, and that distance is reached. Neighbour relations are mutual: if u is t's neighbour in one direction, t is u's neighbour in the opposite direction.
All inputs are finite; a program needn't handle non-finite values. No bound on the sum of `land_mask` on one device may be relied on, other than what follows from the above.
Results may differ from the reference program's by a relative error of at most 0.0063.
Values may be sent and summed in bfloat16 or wider, within the bound.
No kernel may reach another device: no remote copies, remote signals or barrier semaphores. Data moves between devices by JAX's collectives and lax.ppermute only.
A program may use at most 128 MiB of HBM per device.

```python
import math
import jax
import jax.numpy as jnp
from jax import lax

C = 128
FF = 512
TS = 64
TILES_DEV = 2
HALO = 3
KK = 49
CELLS = 4096
TILES = 32


def draw_neighbours(key, part):
    base_key = jax.random.fold_in(key, 7)
    count_key, order_key = jax.random.split(base_key)
    columns = TILES
    grid_rows = 2 * TILES_DEV
    wanted = jax.random.randint(count_key, (columns,), 1, TILES_DEV + 1)
    wanted = wanted.at[0].set(TILES_DEV - 1).at[1].set(TILES_DEV).at[2].set(TILES_DEV)
    starts = jnp.cumsum(wanted) - wanted
    counts = jnp.clip(TILES - starts, 0, wanted)
    column_keys = jax.random.split(order_key, columns)
    row_order = jax.vmap(lambda column_key: jax.random.permutation(column_key, grid_rows))(column_keys)
    is_ocean = row_order < counts[:, None]
    row_ids = jnp.arange(grid_rows)
    is_ocean = is_ocean.at[1].set((row_ids >= 1) & (row_ids <= TILES_DEV))
    is_ocean = is_ocean.at[2].set(row_ids < TILES_DEV)
    row_rank = jnp.cumsum(is_ocean.astype(jnp.int32), axis=1) - 1
    slot_ids = starts[:, None] + row_rank
    padded_ocean = jnp.pad(is_ocean, 1)
    padded_slots = jnp.pad(slot_ids, 1)
    offsets = ((0, -1), (0, 1), (-1, 0), (1, 0), (-1, -1), (1, -1), (-1, 1), (1, 1))
    entries = []
    for col_step, row_step in offsets:
        neighbour_ocean = padded_ocean[1 + col_step:1 + col_step + columns, 1 + row_step:1 + row_step + grid_rows]
        neighbour_slot = padded_slots[1 + col_step:1 + col_step + columns, 1 + row_step:1 + row_step + grid_rows]
        entries.append(jnp.where(neighbour_ocean, neighbour_slot, -1))
    grid_table = jnp.stack(entries, -1).astype(jnp.int32)
    target = jnp.where(is_ocean, slot_ids, TILES).reshape(-1)
    neighbour_table = jnp.full((TILES, 8), -1, jnp.int32)
    return neighbour_table.at[target].set(grid_table.reshape(-1, 8), mode='drop')


def touch_ends(array, stream_key, least, largest):
    spot = [jax.random.randint(jax.random.fold_in(stream_key, axis), (), 0, length) for axis, length in enumerate(array.shape)]
    longest = array.shape.index(max(array.shape))
    beside = spot[:longest] + [(spot[longest] + 1) % array.shape[longest]] + spot[longest + 1:]
    return array.at[tuple(spot)].set(least).at[tuple(beside)].set(largest)


def level_of(key, dims, shards, least, largest):
    def one(axis_at, shards_of):
        heights = jax.random.uniform(jax.random.fold_in(jax.random.fold_in(key, 6), axis_at), (shards_of,), jnp.float32, least / len(shards), largest / len(shards))
        return jnp.repeat(jnp.exp(heights), dims[axis_at] // shards_of).reshape((-1,) + (1,) * (len(dims) - axis_at - 1))

    loudness = one(*shards[0])
    for cut in shards[1:]:
        loudness = loudness * one(*cut)
    return loudness


def normal_values(rng, dims, deviation, limit, cuts=(), kind=jnp.bfloat16):
    array = deviation * jax.random.normal(rng, dims, jnp.float32)
    if cuts:
        array = array * level_of(rng, dims, cuts, -0.22, 0.18)
    return jnp.clip(array, -limit, limit).astype(kind)


def setup_inputs(seed: int = 0, part: int = 0) -> dict:
    key_of = jax.random.split(jax.random.key(seed), 14)
    part_splits = jax.random.split(jax.random.fold_in(key_of[13], part), 14)
    return {
        "tile_state": normal_values(part_splits[0], (TILES, TS, TS, C), 1.0, 6.0, ((0, 16),)),
        "cotangent": normal_values(part_splits[1], (TILES, TS, TS, C), 1.0, 6.0, ((0, 16),)),
        "neighbours": draw_neighbours(jax.random.fold_in(jax.random.fold_in(key_of[13], part), 71), part),
        "land_mask": touch_ends((jax.random.randint(part_splits[3], (TILES, CELLS), 0, 5) < 4).astype(jnp.int32), jax.random.fold_in(part_splits[3], 1), 0, 1),
        "kernel": normal_values(key_of[4], (KK, C), KK ** -0.5, 0.875, (), jnp.float32),
        "conv_bias": normal_values(key_of[5], (C,), 0.5, 3.0, (), jnp.float32),
        "norm_gain": jnp.clip(1.0 + 0.15 * jax.random.normal(key_of[6], (C,), jnp.float32), 0.25, 1.75),
        "norm_bias": normal_values(key_of[7], (C,), 0.4, 3.0, (), jnp.float32),
        "w_up": normal_values(key_of[8], (FF, C), C ** -0.5, 0.5),
        "up_bias": normal_values(key_of[9], (FF,), 0.5, 3.0, (), jnp.float32),
        "w_down": normal_values(key_of[10], (FF, C), FF ** -0.5, 0.25),
        "down_bias": normal_values(key_of[11], (C,), 0.5, 3.0, (), jnp.float32),
        "layer_scale": jnp.clip(jnp.exp(jax.random.uniform(key_of[12], (C,), jnp.float32, math.log(0.3), math.log(1.0))), 0.3, 1.0),
    }


EPSILON = 1e-06
INV_SQRT2 = 0.7071067811865476
INV_SQRT2PI = 0.3989422804014327

def band_stack(field, halo):
    edge = field.shape[1]
    top_rows = field[:, :halo]
    bottom_rows = field[:, edge - halo:]
    left_cols = jnp.swapaxes(field[:, :, :halo], 1, 2)
    right_cols = jnp.swapaxes(field[:, :, edge - halo:], 1, 2)
    return jnp.stack([top_rows, bottom_rows, left_cols, right_cols], 1)

def pick(band_table, local_slot, present, direction, which):
    chosen = band_table[local_slot[:, direction], which]
    return jnp.where(present[:, direction][:, None, None, None], chosen, jnp.zeros((), chosen.dtype))

def assemble(own_tiles, band_table, local_slot, present, halo):
    edge = own_tiles.shape[1]
    north = pick(band_table, local_slot, present, 0, 1)
    south = pick(band_table, local_slot, present, 1, 0)
    west = jnp.swapaxes(pick(band_table, local_slot, present, 2, 3), 1, 2)
    east = jnp.swapaxes(pick(band_table, local_slot, present, 3, 2), 1, 2)
    corner_nw = pick(band_table, local_slot, present, 4, 1)[:, :, edge - halo:]
    corner_ne = pick(band_table, local_slot, present, 5, 1)[:, :, :halo]
    corner_sw = pick(band_table, local_slot, present, 6, 0)[:, :, edge - halo:]
    corner_se = pick(band_table, local_slot, present, 7, 0)[:, :, :halo]
    upper = jnp.concatenate([corner_nw, north, corner_ne], 2)
    middle = jnp.concatenate([west, own_tiles, east], 2)
    lower = jnp.concatenate([corner_sw, south, corner_se], 2)
    return jnp.concatenate([upper, middle, lower], 1)

def depthwise(padded, kernel):
    ksize = math.isqrt(kernel.shape[0])
    chans = kernel.shape[1]
    weights = kernel.reshape(ksize, ksize, 1, chans)
    return lax.conv_general_dilated(padded, weights, (1, 1), 'VALID', dimension_numbers=('NHWC', 'HWIO', 'NHWC'), feature_group_count=chans, precision=lax.Precision.HIGHEST)

def piece_stack(d_padded, halo):
    edge = d_padded.shape[1] - 2 * halo
    stop = halo + edge
    north = d_padded[:, :halo, halo:stop]
    south = d_padded[:, stop:, halo:stop]
    west = jnp.swapaxes(d_padded[:, halo:stop, :halo], 1, 2)
    east = jnp.swapaxes(d_padded[:, halo:stop, stop:], 1, 2)
    edges = jnp.stack([south, north, east, west], 1)
    corners = jnp.stack([d_padded[:, :halo, :halo], d_padded[:, :halo, stop:], d_padded[:, stop:, :halo], d_padded[:, stop:, stop:]], 1)
    return (d_padded[:, halo:stop, halo:stop], edges, corners)

def collect(interior, edge_table, corner_table, local_slot, present, halo):
    edge = interior.shape[1]
    low = edge - halo
    total = interior.at[:, :halo].add(pick(edge_table, local_slot, present, 0, 0))
    total = total.at[:, low:].add(pick(edge_table, local_slot, present, 1, 1))
    total = total.at[:, :, :halo].add(jnp.swapaxes(pick(edge_table, local_slot, present, 2, 2), 1, 2))
    total = total.at[:, :, low:].add(jnp.swapaxes(pick(edge_table, local_slot, present, 3, 3), 1, 2))
    total = total.at[:, :halo, :halo].add(pick(corner_table, local_slot, present, 4, 3))
    total = total.at[:, :halo, low:].add(pick(corner_table, local_slot, present, 5, 2))
    total = total.at[:, low:, :halo].add(pick(corner_table, local_slot, present, 6, 1))
    total = total.at[:, low:, low:].add(pick(corner_table, local_slot, present, 7, 0))
    return total

def tile_mlp(conv_rows, state_rows, cot_rows, mask_rows, w_up, up_bias, w_down, down_bias, norm_gain, norm_bias, layer_scale):
    centred = conv_rows - lax.optimization_barrier(jnp.mean(conv_rows, axis=-1, keepdims=True))
    inv_std = lax.rsqrt(lax.optimization_barrier(jnp.mean(centred * centred, axis=-1, keepdims=True)) + EPSILON)
    normal = centred * inv_std
    hidden = (normal * norm_gain + norm_bias).astype(jnp.bfloat16)
    pre = lax.dot_general(hidden, w_up, (((1,), (1,)), ((), ())), preferred_element_type=jnp.float32) + up_bias
    cumul = 0.5 * (1.0 + jax.scipy.special.erf(pre * INV_SQRT2))
    slope = cumul + pre * jnp.exp(-0.5 * pre * pre) * INV_SQRT2PI
    act = (pre * cumul).astype(jnp.bfloat16)
    branch = jnp.dot(act, w_down, preferred_element_type=jnp.float32) + down_bias
    output = (state_rows + mask_rows * layer_scale * branch).astype(jnp.bfloat16)
    d_branch = cot_rows * mask_rows * layer_scale
    grad_scale_part = lax.optimization_barrier(jnp.sum(cot_rows * mask_rows * branch, 0))
    d_branch_b = d_branch.astype(jnp.bfloat16)
    grad_down_part = lax.dot_general(act, d_branch_b, (((0,), (0,)), ((), ())), preferred_element_type=jnp.float32)
    d_act = lax.dot_general(d_branch_b, w_down, (((1,), (1,)), ((), ())), preferred_element_type=jnp.float32)
    d_pre = d_act * slope
    d_pre_b = d_pre.astype(jnp.bfloat16)
    grad_up_part = lax.dot_general(d_pre_b, hidden, (((0,), (0,)), ((), ())), preferred_element_type=jnp.float32)
    d_hidden = jnp.dot(d_pre_b, w_up, preferred_element_type=jnp.float32)
    d_normal = d_hidden * norm_gain
    d_conv = inv_std * (d_normal - lax.optimization_barrier(jnp.mean(d_normal, axis=-1, keepdims=True)) - normal * lax.optimization_barrier(jnp.mean(d_normal * normal, axis=-1, keepdims=True)))
    vector_part = jnp.stack([lax.optimization_barrier(jnp.sum(d_conv, 0)), lax.optimization_barrier(jnp.sum(d_hidden * normal, 0)), lax.optimization_barrier(jnp.sum(d_hidden, 0)), lax.optimization_barrier(jnp.sum(d_branch, 0)), grad_scale_part])
    return (output, d_conv, grad_up_part, grad_down_part, lax.optimization_barrier(jnp.sum(d_pre, 0)), vector_part)

def reference(tile_state, cotangent, neighbours, land_mask, kernel, conv_bias, norm_gain, norm_bias, w_up, up_bias, w_down, down_bias, layer_scale):
    tiles, edge, chans = (tile_state.shape[0], tile_state.shape[1], tile_state.shape[3])
    cells = edge * edge
    mask_cells = land_mask.reshape(tiles, edge, edge, 1)
    masked = tile_state * mask_cells.astype(jnp.bfloat16)
    band_table = band_stack(masked, HALO)
    present = neighbours >= 0
    local_slot = jnp.where(present, neighbours, 0).astype(jnp.int32)

    def per_tile(totals, items):
        own_tile, slot_row, present_row, state_rows, cot_rows, mask_rows = items
        padded = assemble(own_tile[None], band_table, slot_row[None], present_row[None], HALO).astype(jnp.float32)
        conv_out, conv_back = jax.vjp(depthwise, padded, kernel)
        conv_rows = conv_out.reshape(cells, chans) + conv_bias
        output, d_conv, up_part, down_part, upbias_part, vector_part = tile_mlp(conv_rows, state_rows.astype(jnp.float32), cot_rows.astype(jnp.float32), mask_rows, w_up, up_bias, w_down, down_bias, norm_gain, norm_bias, layer_scale)
        d_padded, kernel_part = conv_back(d_conv.reshape(conv_out.shape))
        interior, edges, corners = piece_stack(d_padded, HALO)
        totals = (totals[0] + up_part, totals[1] + down_part, totals[2] + upbias_part, totals[3] + vector_part, totals[4] + kernel_part)
        return (totals, (output, interior[0], edges[0], corners[0]))
    start = (jnp.zeros((FF, chans), jnp.float32), jnp.zeros((FF, chans), jnp.float32), jnp.zeros((FF,), jnp.float32), jnp.zeros((5, chans), jnp.float32), jnp.zeros(kernel.shape, jnp.float32))
    items = (masked, local_slot, present, tile_state.reshape(tiles, cells, chans), cotangent.reshape(tiles, cells, chans), land_mask.reshape(tiles, cells, 1).astype(jnp.float32))
    totals, (outputs, interiors, edge_table, corner_table) = lax.scan(per_tile, start, items)
    d_masked = collect(interiors, edge_table, corner_table, local_slot, present, HALO)
    grad_state = (cotangent.astype(jnp.float32) + mask_cells.astype(jnp.float32) * d_masked).astype(jnp.bfloat16)
    block_out = outputs.reshape(tiles, edge, edge, chans)
    return (block_out, grad_state, totals[0], totals[1], totals[4], totals[3], totals[2])
```

```python
import functools

import jax
import jax.numpy as jnp
from jax import lax
from jax.experimental import pallas as pl
from jax.experimental.pallas import tpu as pltpu
from jax.sharding import PartitionSpec as P

REACH = 2
HALO = 3
KSIZE = 7
TAPS = KSIZE * KSIZE
ROWS = 8
CONV_ROWS = 16
FCHUNK = 256
CELLS = 256
STEP_ROWS = 16
VMEM_MIB = 58

EPSILON = 1e-06
INV_SQRT2 = 0.7071067811865476
INV_SQRT2PI = 0.3989422804014327
LOG2E = 1.4426950408889634

F32 = jnp.float32
BF16 = jnp.bfloat16
NT = (((1,), (1,)), ((), ()))


def shifted(shard, axis, by):
    count = lax.axis_size(axis)
    pairs = [(i, i + by) for i in range(count) if 0 <= i + by < count]
    return lax.ppermute(shard, axis, pairs)


def params(limit_mib, side=False):
    return pltpu.CompilerParams(vmem_limit_bytes=limit_mib << 20)


def spread(rows, chans):
    height = rows.shape[0]
    row = lax.broadcasted_iota(jnp.int32, (height, height * chans), 0)
    lane = lax.broadcasted_iota(jnp.int32, (height, height * chans), 1)
    pick = ((lane >= row * chans) & (lane < (row + 1) * chans)).astype(F32).astype(BF16)
    wide = jnp.dot(rows.T.astype(BF16), pick, preferred_element_type=F32)
    return [wide[:, r * chans : (r + 1) * chans] for r in range(height)]


def bands_kernel(state_ref, mask_ref, out_ref, left, right):
    edge = state_ref.shape[1]
    low = edge - HALO
    upper = mask_ref[0, 0:8].T
    lower = mask_ref[0, edge - 8 :].T
    for q in range(HALO):
        out_ref[0, 0, q] = (state_ref[0, q].astype(F32) * upper[:, q : q + 1]).astype(BF16)
        p = 8 - HALO + q
        out_ref[0, 1, q] = (state_ref[0, low + q].astype(F32) * lower[:, p : p + 1]).astype(BF16)
    left[...] = state_ref[0, :, 0:16].astype(F32).reshape(left.shape)
    right[...] = state_ref[0, :, edge - 16 :].astype(F32).reshape(right.shape)
    for q in range(HALO):
        out_ref[0, 2, q] = (
            left[pl.ds(q, edge, stride=16), :] * mask_ref[0, :, q : q + 1]
        ).astype(BF16)
        out_ref[0, 3, q] = (
            right[pl.ds(16 - HALO + q, edge, stride=16), :] * mask_ref[0, :, low + q : low + q + 1]
        ).astype(BF16)


def bands_call(state, mask):
    slots, edge, _, chans = state.shape
    return pl.pallas_call(
        bands_kernel,
        grid=(slots,),
        in_specs=[
            pl.BlockSpec((1, edge, edge, chans), lambda s: (s, 0, 0, 0)),
            pl.BlockSpec((1, edge, edge), lambda s: (s, 0, 0)),
        ],
        out_specs=pl.BlockSpec((1, 4, HALO, edge, chans), lambda s: (s, 0, 0, 0, 0)),
        out_shape=jax.ShapeDtypeStruct((slots, 4, HALO, edge, chans), BF16),
        scratch_shapes=[pltpu.VMEM((edge * 16, chans), F32)] * 2,
        compiler_params=params(VMEM_MIB),
        name="bands",
    )(state, mask)


def tap(weight_ref, index, chans):
    return jnp.broadcast_to(weight_ref[index : index + 1, :], (8, chans))


def conv_rows(padded, weight_ref, row, column, write, chans):
    totals = [None] * CONV_ROWS
    for b in range(KSIZE):
        weights = [tap(weight_ref, a * KSIZE + b, chans) for a in range(KSIZE)]
        for r in range(CONV_ROWS + KSIZE - 1):
            cells = padded[row + r, pl.ds(column + b, 8), :]
            for a in range(KSIZE):
                i = r - a
                if 0 <= i < CONV_ROWS:
                    term = cells * weights[a]
                    totals[i] = term if totals[i] is None else totals[i] + term
    for i in range(CONV_ROWS):
        write(i, totals[i])


def zero_margins(padded):
    rows, cols, chans = padded.shape
    padded[0:HALO] = jnp.zeros((HALO, cols, chans), F32)
    padded[rows - HALO :] = jnp.zeros((HALO, cols, chans), F32)

    def body(r, carry):
        padded[r, 0:8] = jnp.zeros((8, chans), F32)
        padded[r, cols - 8 :] = jnp.zeros((8, chans), F32)
        return carry

    lax.fori_loop(HALO, rows - HALO, body, 0)


def fill_masked(padded, state_ref, mask_ref):
    edge, chans = state_ref.shape[1], state_ref.shape[3]

    def body(n, carry):
        slabs = spread(mask_ref[0, pl.ds(pl.multiple_of(n * 8, 8), 8)], chans)
        for r in range(8):
            i = n * 8 + r
            padded[HALO + i, HALO : HALO + edge] = state_ref[0, i].astype(F32) * slabs[r]
        return carry

    lax.fori_loop(0, edge // 8, body, 0, unroll=4)


def conv_tile(padded, weight_ref, out_ref):
    edge, chans = out_ref.shape[1], out_ref.shape[3]

    def body(n, carry):
        for g in range(edge // 8):

            def write(i, value):
                out_ref[0, n * CONV_ROWS + i, g * 8 : g * 8 + 8] = value

            conv_rows(padded, weight_ref, n * CONV_ROWS, g * 8, write, chans)
        return carry

    lax.fori_loop(0, edge // CONV_ROWS, body, 0)


def own_conv_kernel(state_ref, mask_ref, weight_ref, out_ref, padded):
    zero_margins(padded)
    fill_masked(padded, state_ref, mask_ref)
    conv_tile(padded, weight_ref, out_ref)


def padded_shape(edge, chans):
    return (edge + 2 * HALO, edge + 8, chans)


def conv_cost(slots, edge, chans):
    cells = slots * edge * edge * chans
    return pl.CostEstimate(flops=2 * TAPS * cells, bytes_accessed=8 * cells, transcendentals=0)


def own_conv_call(state, mask, weights):
    slots, edge, _, chans = state.shape
    return pl.pallas_call(
        own_conv_kernel,
        grid=(slots,),
        in_specs=[
            pl.BlockSpec((1, edge, edge, chans), lambda s: (s, 0, 0, 0)),
            pl.BlockSpec((1, edge, edge), lambda s: (s, 0, 0)),
            pl.BlockSpec((TAPS, chans), lambda s: (0, 0)),
        ],
        out_specs=pl.BlockSpec((1, edge, edge, chans), lambda s: (s, 0, 0, 0)),
        out_shape=jax.ShapeDtypeStruct((slots, edge, edge, chans), F32),
        scratch_shapes=[pltpu.VMEM(padded_shape(edge, chans), F32)],
        compiler_params=params(VMEM_MIB),
        cost_estimate=conv_cost(slots, edge, chans),
        name="own_conv",
    )(state, mask, weights)


def load_window(sources, window, sem):
    slots = sources[0].shape[0]
    copies = [
        pltpu.make_async_copy(source, window.at[pl.ds(k * slots, slots)], sem.at[k])
        for k, source in enumerate(sources)
    ]
    for copy in copies:
        copy.start()
    for copy in copies:
        copy.wait()


def picked(window, slot_ref, here_ref, tile, direction, which, q):
    band = window[slot_ref[tile, direction], which, q].astype(F32)
    return jnp.where(here_ref[tile, direction] > 0, band, jnp.zeros_like(band))


def fill_rows(north, south, window, slot_ref, here_ref, tile):
    edge = window.shape[3]
    low = edge - HALO
    for q in range(HALO):
        for target, edge_dir, which, left_dir, right_dir in (
            (north, 0, 1, 4, 5),
            (south, 1, 0, 6, 7),
        ):
            target[q, HALO : HALO + edge] = picked(
                window, slot_ref, here_ref, tile, edge_dir, which, q
            )
            target[q, 0:HALO] = picked(window, slot_ref, here_ref, tile, left_dir, which, q)[low:]
            target[q, HALO + edge : HALO + edge + HALO] = picked(
                window, slot_ref, here_ref, tile, right_dir, which, q
            )[0:HALO]


def fill_columns(west, east, window, slot_ref, here_ref, tile):
    edge = window.shape[3]
    for q in range(HALO):
        west[pl.ds(HALO * 16 + q, edge, stride=16), :] = picked(
            window, slot_ref, here_ref, tile, 2, 3, q
        )
        east[pl.ds(HALO * 16 + 8 + HALO + q, edge, stride=16), :] = picked(
            window, slot_ref, here_ref, tile, 3, 2, q
        )


def fill_margins(padded, window, slot_ref, here_ref, tile):
    rows, stride, chans = padded.shape
    edge = window.shape[3]
    fill_rows(padded.at[0:HALO], padded.at[HALO + edge :], window, slot_ref, here_ref, tile)
    flat = padded.reshape(rows * stride, chans)
    for q in range(HALO):
        flat[pl.ds(HALO * stride + q, edge, stride=stride), :] = picked(
            window, slot_ref, here_ref, tile, 2, 3, q
        )
        flat[pl.ds(HALO * stride + HALO + edge + q, edge, stride=stride), :] = picked(
            window, slot_ref, here_ref, tile, 3, 2, q
        )


def clear_margins(north, south, west, east):
    for ref in (north, south, west, east):
        ref[...] = jnp.zeros_like(ref)


def add_columns(west, east, weight_ref, row, target, base, chans):
    edge = target.shape[1]
    for source, first, taps in ((west, 0, range(HALO)), (east, edge - 8, range(HALO + 1, KSIZE))):
        totals = [target[base + i, first : first + 8] for i in range(ROWS)]
        for b in taps:
            weights = [tap(weight_ref, a * KSIZE + b, chans) for a in range(KSIZE)]
            for r in range(ROWS + KSIZE - 1):
                cells = source[pl.ds((row + r) * 16 + b, 8), :]
                for a in range(KSIZE):
                    i = r - a
                    if 0 <= i < ROWS:
                        totals[i] = totals[i] + cells * weights[a]
        for i in range(ROWS):
            target[base + i, first : first + 8] = totals[i]


def add_rows(source, weight_ref, target, upper, chans):
    height, edge = target.shape[0], target.shape[1]
    pairs = []
    for q in range(HALO):
        for a in range(KSIZE):
            i = q - a if upper else HALO + q + height - a
            if 0 <= i < height:
                pairs.append((q, a, i))
    for g in range(edge // 8):
        rows = sorted({i for _, _, i in pairs})
        totals = {i: target[i, g * 8 : g * 8 + 8] for i in rows}
        for b in range(KSIZE):
            for q in range(HALO):
                cells = source[q, pl.ds(g * 8 + b, 8), :]
                for p, a, i in pairs:
                    if p == q:
                        totals[i] = totals[i] + cells * tap(weight_ref, a * KSIZE + b, chans)
        for i in rows:
            target[i, g * 8 : g * 8 + 8] = totals[i]


def window_scratch(slots, edge, chans):
    return [
        pltpu.VMEM(((2 * REACH + 1) * slots, 4, HALO, edge, chans), BF16),
        pltpu.SemaphoreType.DMA((2 * REACH + 1,)),
    ]


def margin_scratch(slots, edge, chans):
    return window_scratch(slots, edge, chans) + [
        pltpu.VMEM((HALO, edge + 8, chans), F32),
        pltpu.VMEM((HALO, edge + 8, chans), F32),
        pltpu.VMEM(((edge + 2 * HALO) * 16, chans), F32),
        pltpu.VMEM(((edge + 2 * HALO) * 16, chans), F32),
    ]


def margin_setup(sources, slot_ref, here_ref, scratch):
    window, sem, north, south, west, east = scratch
    tile, block = pl.program_id(0), pl.program_id(1)

    @pl.when((tile == 0) & (block == 0))
    def _():
        load_window(sources, window, sem)
        clear_margins(north, south, west, east)

    @pl.when(block == 0)
    def _():
        fill_rows(north, south, window, slot_ref, here_ref, tile)
        fill_columns(west, east, window, slot_ref, here_ref, tile)


def margin_add(weight_ref, target, scratch, chans):
    _, _, north, south, west, east = scratch
    block, blocks = pl.program_id(1), pl.num_programs(1)
    height = target.shape[0]

    def body(n, carry):
        add_columns(west, east, weight_ref, block * height + n * ROWS, target, n * ROWS, chans)
        return carry

    lax.fori_loop(0, height // ROWS, body, 0)

    @pl.when(block == 0)
    def _():
        add_rows(north, weight_ref, target, True, chans)

    @pl.when(block == blocks - 1)
    def _():
        add_rows(south, weight_ref, target, False, chans)


def folded(values):
    cells, chans = values.shape
    return jnp.sum(values.reshape(cells // 8, 8, chans), 0)


def mlp_cells(parts, par, acc):
    bias, gain, nbias, wup, upb, wdown, dbias, scale, wup_t, wdown_t = par
    gup, gdown, upacc, vec = acc
    units = wup.shape[0]
    chans = wup.shape[1]
    upper = []
    for conv, cot, mask in parts:
        conv = conv + bias[...]
        centred = conv - jnp.mean(conv, axis=-1, keepdims=True)
        inv_std = lax.rsqrt(jnp.mean(centred * centred, axis=-1, keepdims=True) + EPSILON)
        normal = centred * inv_std
        hidden = (normal * gain[...] + nbias[...]).astype(BF16)
        cotm = cot * mask
        dbranch = cotm * scale[...]
        upper.append((normal, inv_std, hidden, cotm, dbranch, dbranch.astype(BF16)))
    acts, dpres = [], []
    for f in range(0, units, FCHUNK):
        part = slice(f, f + FCHUNK)
        total = upacc[part]
        for _, _, hidden, _, _, dbranch_b in upper:
            cells = hidden.shape[0]
            pre = lax.dot_general(wup[part], hidden, NT, preferred_element_type=F32)
            pre = pre + jnp.concatenate([upb[part]] * (cells // 128), 1)
            dact = lax.dot_general(wdown[part], dbranch_b, NT, preferred_element_type=F32)
            cumul = 0.5 + 0.5 * lax.erf(pre * INV_SQRT2)
            slope = cumul + pre * (jnp.exp(-0.5 * pre * pre) * INV_SQRT2PI)
            dpre = dact * slope
            acts.append((pre * cumul).astype(BF16))
            dpres.append(dpre.astype(BF16))
            for lane in range(0, cells, 128):
                total = total + dpre[:, lane : lane + 128]
        upacc[part] = total
    count = len(parts)
    results = []
    sums = [vec[k] for k in range(5)]
    ups, downs = [], []
    for h, (normal, inv_std, hidden, cotm, dbranch, dbranch_b) in enumerate(upper):
        act = jnp.concatenate(acts[h::count], 0)
        dpre_b = jnp.concatenate(dpres[h::count], 0)
        ups.append(jnp.dot(dpre_b, hidden, preferred_element_type=F32))
        downs.append(jnp.dot(act, dbranch_b, preferred_element_type=F32))
        branch = jnp.dot(wdown_t[...], act, preferred_element_type=F32).T + dbias[...]
        dhidden = jnp.dot(wup_t[...], dpre_b, preferred_element_type=F32).T
        dnormal = dhidden * gain[...]
        dconv = inv_std * (
            dnormal
            - jnp.mean(dnormal, axis=-1, keepdims=True)
            - normal * jnp.mean(dnormal * normal, axis=-1, keepdims=True)
        )
        for k, values in enumerate((dconv, dhidden * normal, dhidden, dbranch, cotm * branch)):
            sums[k] = sums[k] + folded(values)
        results.append((branch, dconv))
    gup[...] += sum(ups[1:], ups[0])
    gdown[...] += sum(downs[1:], downs[0])
    for k in range(5):
        vec[k] = sums[k]
    return results


def mlp_kernel(slot_ref, here_ref, *refs):
    sources = refs[:5]
    conv_ref, state_ref, cot_ref, mask_ref, weight_ref = refs[5:10]
    bias, gain, nbias, wup, upb, wdown, dbias, scale = refs[10:18]
    out_ref, grad_ref, bands_ref, gup, gdown, upacc, vec = refs[18:25]
    conv_s, tile_grad, wup_t, wdown_t, upb_s = refs[25:30]
    scratch = refs[30:]
    par = (bias, gain, nbias, wup, upb_s, wdown, dbias, scale, wup_t, wdown_t)
    tile, block, blocks = pl.program_id(0), pl.program_id(1), pl.num_programs(1)
    height, edge, chans = conv_s.shape
    low = edge - HALO

    @pl.when((tile == 0) & (block == 0))
    def _():
        for ref in (gup, gdown, upacc, vec):
            ref[...] = jnp.zeros_like(ref)
        wup_t[...] = wup[...].astype(F32).T.astype(BF16)
        wdown_t[...] = wdown[...].astype(F32).T.astype(BF16)
        upb_s[...] = jnp.broadcast_to(upb[...], (128, upb.shape[1])).T

    margin_setup(sources, slot_ref, here_ref, scratch)
    conv_s[...] = conv_ref[0]
    margin_add(weight_ref, conv_s, scratch, chans)
    rows = CELLS // edge

    def body(n, carry):
        slabs = spread(mask_ref[0, pl.ds(pl.multiple_of(n * ROWS, ROWS), ROWS)], chans)
        parts, places, masks = [], [], []
        for h in range(ROWS // rows):
            first = n * ROWS + h * rows
            place = pl.ds(first, rows)
            mask = jnp.concatenate(slabs[h * rows : (h + 1) * rows], 0)
            places.append((first, place))
            masks.append(mask)
            parts.append(
                (
                    conv_s[place].reshape(CELLS, chans),
                    cot_ref[0, place].astype(F32).reshape(CELLS, chans),
                    mask,
                )
            )
        results = mlp_cells(parts, par, (gup, gdown, upacc, vec))
        for (first, place), mask, (branch, dconv) in zip(places, masks, results):
            state = state_ref[0, place].astype(F32).reshape(CELLS, chans)
            output = (state + (mask * scale[...]) * branch).astype(BF16)
            out_ref[0, place] = output.reshape(rows, edge, chans)
            grad_ref[0, place] = dconv.reshape(rows, edge, chans)
            start = pl.multiple_of((block * height + first) * edge, CELLS)
            tile_grad[pl.ds(start, CELLS), :] = dconv
        return carry

    lax.fori_loop(0, height // ROWS, body, 0)

    @pl.when(block == blocks - 1)
    def _():
        for q in range(HALO):
            bands_ref[0, 0, q] = tile_grad[q * edge : (q + 1) * edge].astype(BF16)
            bands_ref[0, 1, q] = tile_grad[(low + q) * edge : (low + q + 1) * edge].astype(BF16)
            bands_ref[0, 2, q] = tile_grad[pl.ds(q, edge, stride=edge), :].astype(BF16)
            bands_ref[0, 3, q] = tile_grad[pl.ds(low + q, edge, stride=edge), :].astype(BF16)


def mlp_call(slot, here, sources, conv, state, cot, mask, weights, par):
    slots, edge, _, chans = state.shape
    units = par[3].shape[0]
    blocks = edge // STEP_ROWS
    row_spec = pl.BlockSpec((1, STEP_ROWS, edge, chans), lambda s, n, *_: (s, n, 0, 0))

    def whole(a):
        return pl.BlockSpec(a.shape, lambda s, n, *_: (0,) * a.ndim)

    grid_spec = pltpu.PrefetchScalarGridSpec(
        num_scalar_prefetch=2,
        grid=(slots, blocks),
        in_specs=[pl.BlockSpec(memory_space=pl.ANY)] * 5
        + [
            row_spec,
            row_spec,
            row_spec,
            pl.BlockSpec((1, STEP_ROWS, edge), lambda s, n, *_: (s, n, 0)),
            whole(weights),
        ]
        + [whole(a) for a in par],
        out_specs=[
            row_spec,
            row_spec,
            pl.BlockSpec((1, 4, HALO, edge, chans), lambda s, n, *_: (s, 0, 0, 0, 0)),
            pl.BlockSpec((units, chans), lambda s, n, *_: (0, 0)),
            pl.BlockSpec((units, chans), lambda s, n, *_: (0, 0)),
            pl.BlockSpec((units, 128), lambda s, n, *_: (0, 0)),
            pl.BlockSpec((5, 8, chans), lambda s, n, *_: (0, 0, 0)),
        ],
        scratch_shapes=[
            pltpu.VMEM((STEP_ROWS, edge, chans), F32),
            pltpu.VMEM((edge * edge, chans), F32),
            pltpu.VMEM((chans, units), BF16),
            pltpu.VMEM((chans, units), BF16),
            pltpu.VMEM((units, 128), F32),
        ]
        + margin_scratch(slots, edge, chans),
    )
    cells = slots * edge * edge
    return pl.pallas_call(
        mlp_kernel,
        grid_spec=grid_spec,
        out_shape=[
            jax.ShapeDtypeStruct(state.shape, BF16),
            jax.ShapeDtypeStruct(state.shape, F32),
            jax.ShapeDtypeStruct((slots, 4, HALO, edge, chans), BF16),
            jax.ShapeDtypeStruct((units, chans), F32),
            jax.ShapeDtypeStruct((units, chans), F32),
            jax.ShapeDtypeStruct((units, 128), F32),
            jax.ShapeDtypeStruct((5, 8, chans), F32),
        ],
        compiler_params=params(VMEM_MIB),
        cost_estimate=pl.CostEstimate(
            flops=12 * cells * units * chans, bytes_accessed=14 * cells * chans, transcendentals=0
        ),
        name="mlp",
    )(slot, here, *sources, conv, state, cot, mask, weights, *par)


def tap_grad_kernel(slot_ref, here_ref, *refs):
    sources = refs[:5]
    state_ref, mask_ref, grad_ref, upacc, vec, out_ref = refs[5:11]
    padded, totals, small = refs[11:14]
    window, sem = refs[14:]
    tile, tiles = pl.program_id(0), pl.num_programs(0)
    edge, chans = grad_ref.shape[1], grad_ref.shape[3]

    @pl.when(tile == 0)
    def _():
        load_window(sources, window, sem)
        totals[...] = jnp.zeros_like(totals)
        zero_margins(padded)

    fill_masked(padded, state_ref, mask_ref)
    fill_margins(padded, window, slot_ref, here_ref, tile)

    for b in range(KSIZE):

        def body(n, sums, b=b):
            sums = list(sums)
            row = n * ROWS
            for g in range(edge // 8):
                grads = [grad_ref[0, row + i, g * 8 : g * 8 + 8] for i in range(ROWS)]
                for r in range(ROWS + KSIZE - 1):
                    cells = padded[row + r, pl.ds(g * 8 + b, 8), :]
                    for a in range(KSIZE):
                        if 0 <= r - a < ROWS:
                            sums[a] = sums[a] + cells * grads[r - a]
            return tuple(sums)

        start = tuple(totals[a * KSIZE + b] for a in range(KSIZE))
        sums = lax.fori_loop(0, edge // ROWS, body, start)
        for a in range(KSIZE):
            totals[a * KSIZE + b] = sums[a]

    @pl.when(tile == tiles - 1)
    def _():
        small[...] = jnp.zeros_like(small)
        small[0:TAPS] = jnp.sum(totals[...], 1)
        small[TAPS : TAPS + 5] = jnp.sum(vec[...], 1)
        units = upacc.shape[0]
        for u in range(units // 128):
            small[TAPS + 5 + u : TAPS + 6 + u] = jnp.sum(
                upacc[u * 128 : (u + 1) * 128].T, 0, keepdims=True
            )
        high = small[...].astype(BF16)
        out_ref[0] = high
        out_ref[1] = (small[...] - high.astype(F32)).astype(BF16)


def tap_grad_call(slot, here, sources, state, mask, grad, upacc, vec):
    slots, edge, _, chans = state.shape
    rows = TAPS + 5 + upacc.shape[0] // 128
    rows = -(-rows // 16) * 16
    tile_spec = pl.BlockSpec((1, edge, edge, chans), lambda s, *_: (s, 0, 0, 0))
    grid_spec = pltpu.PrefetchScalarGridSpec(
        num_scalar_prefetch=2,
        grid=(slots,),
        in_specs=[pl.BlockSpec(memory_space=pl.ANY)] * 5
        + [
            tile_spec,
            pl.BlockSpec((1, edge, edge), lambda s, *_: (s, 0, 0)),
            tile_spec,
            pl.BlockSpec(upacc.shape, lambda s, *_: (0, 0)),
            pl.BlockSpec(vec.shape, lambda s, *_: (0, 0, 0)),
        ],
        out_specs=pl.BlockSpec((2, rows, chans), lambda s, *_: (0, 0, 0)),
        scratch_shapes=[
            pltpu.VMEM(padded_shape(edge, chans), F32),
            pltpu.VMEM((TAPS, 8, chans), F32),
            pltpu.VMEM((rows, chans), F32),
        ]
        + window_scratch(slots, edge, chans),
    )
    return pl.pallas_call(
        tap_grad_kernel,
        grid_spec=grid_spec,
        out_shape=jax.ShapeDtypeStruct((2, rows, chans), BF16),
        compiler_params=params(VMEM_MIB),
        cost_estimate=conv_cost(slots, edge, chans),
        name="tap_grad",
    )(slot, here, *sources, state, mask, grad, upacc, vec)


def state_grad_kernel(slot_ref, here_ref, *refs):
    sources = refs[:5]
    grad_ref, cot_ref, mask_ref, weight_ref, out_ref, padded, conv_s, window, sem = refs[5:]
    tile = pl.program_id(0)
    edge, chans = grad_ref.shape[1], grad_ref.shape[3]

    @pl.when(tile == 0)
    def _():
        load_window(sources, window, sem)
        zero_margins(padded)

    def fill(n, carry):
        for r in range(8):
            i = n * 8 + r
            padded[HALO + i, HALO : HALO + edge] = grad_ref[0, i]
        return carry

    lax.fori_loop(0, edge // 8, fill, 0)
    fill_margins(padded, window, slot_ref, here_ref, tile)

    def body(n, carry):
        row = n * CONV_ROWS
        for g in range(edge // 8):

            def write(i, value):
                conv_s[i, g * 8 : g * 8 + 8] = value

            conv_rows(padded, weight_ref, row, g * 8, write, chans)
        for k in range(0, CONV_ROWS, 8):
            slabs = spread(mask_ref[0, pl.ds(pl.multiple_of(row + k, 8), 8)], chans)
            for r in range(8):
                i = row + k + r
                out_ref[0, i] = (cot_ref[0, i].astype(F32) + slabs[r] * conv_s[k + r]).astype(BF16)
        return carry

    lax.fori_loop(0, edge // CONV_ROWS, body, 0)


def state_grad_call(slot, here, sources, grad, cot, mask, weights):
    slots, edge, _, chans = cot.shape
    tile_spec = pl.BlockSpec((1, edge, edge, chans), lambda s, *_: (s, 0, 0, 0))
    grid_spec = pltpu.PrefetchScalarGridSpec(
        num_scalar_prefetch=2,
        grid=(slots,),
        in_specs=[pl.BlockSpec(memory_space=pl.ANY)] * 5
        + [
            tile_spec,
            tile_spec,
            pl.BlockSpec((1, edge, edge), lambda s, *_: (s, 0, 0)),
            pl.BlockSpec((TAPS, chans), lambda s, *_: (0, 0)),
        ],
        out_specs=tile_spec,
        scratch_shapes=[
            pltpu.VMEM(padded_shape(edge, chans), F32),
            pltpu.VMEM((CONV_ROWS, edge, chans), F32),
        ]
        + window_scratch(slots, edge, chans),
    )
    return pl.pallas_call(
        state_grad_kernel,
        grid_spec=grid_spec,
        out_shape=jax.ShapeDtypeStruct(cot.shape, BF16),
        compiler_params=params(VMEM_MIB),
        cost_estimate=conv_cost(slots, edge, chans),
        name="state_grad",
    )(slot, here, *sources, grad, cot, mask, weights)


def exchange(bands):
    return [
        bands if offset == 0 else shifted(bands, "tx", -offset)
        for offset in range(-REACH, REACH + 1)
    ]


def per_device(
    tile_state,
    cotangent,
    neighbours,
    land_mask,
    kernel,
    conv_bias,
    norm_gain,
    norm_bias,
    w_up,
    up_bias,
    w_down,
    down_bias,
    layer_scale,
):
    slots, edge, chans = (tile_state.shape[0], tile_state.shape[1], tile_state.shape[3])
    units = w_up.shape[0]
    count = lax.axis_size("tx")
    mask = land_mask.reshape(slots, edge, edge).astype(F32)
    first_slot = (lax.axis_index("tx") - REACH) * slots
    here = (neighbours >= 0).astype(jnp.int32)
    slot = jnp.clip(neighbours - first_slot, 0, (2 * REACH + 1) * slots - 1)
    par = (
        conv_bias[None],
        norm_gain[None],
        norm_bias[None],
        w_up,
        up_bias[None],
        w_down,
        down_bias[None],
        layer_scale[None],
    )
    flipped = kernel[::-1]

    window = exchange(bands_call(tile_state, mask))
    conv = own_conv_call(tile_state, mask, kernel)
    block_out, grad, grad_bands, gup, gdown, upacc, vec = mlp_call(
        slot, here, window, conv, tile_state, cotangent, mask, kernel, par
    )
    grad_window = exchange(grad_bands)

    small = tap_grad_call(slot, here, window, tile_state, mask, grad, upacc, vec)
    rows = small.shape[1]
    sums = small.reshape(2 * rows, chans)
    pieces = jnp.concatenate(
        [
            gup.astype(BF16).reshape(count, -1, chans),
            gdown.astype(BF16).reshape(count, -1, chans),
            jnp.broadcast_to(sums[None], (count,) + sums.shape),
        ],
        1,
    )
    pieces, grad_window, grad = lax.optimization_barrier((pieces, grad_window, grad))
    pieces = lax.all_to_all(pieces, "tx", 0, 0, tiled=True)
    totals = jnp.sum(pieces.astype(F32), 0)
    share = units // count
    grads = (totals[:share], totals[share : 2 * share])
    small = totals[2 * share : 2 * share + rows] + totals[2 * share + rows :]

    grad_state = state_grad_call(slot, here, grad_window, grad, cotangent, mask, flipped)

    grad_kernel = small[:TAPS]
    grad_vectors = small[TAPS : TAPS + 5]
    grad_up_bias = small[TAPS + 5 : TAPS + 5 + units // 128].reshape(units)
    return (block_out, grad_state, grads[0], grads[1], grad_kernel, grad_vectors, grad_up_bias)


def solution(mesh):
    tiles = P(("groups", "tx"), None, None, None)
    rows = P(("groups", "tx"), None)
    return jax.shard_map(
        per_device,
        mesh=mesh,
        in_specs=(tiles, tiles, rows, rows) + (P(),) * 9,
        out_specs=(tiles, tiles, rows, rows, P("groups", None), P("groups", None), P("groups")),
        check_vma=False,
    )
```

```python
import functools

import jax
import jax.numpy as jnp
from jax import lax
from jax.experimental import pallas as pl
from jax.experimental.pallas import tpu as pltpu
from jax.sharding import PartitionSpec as P

REACH = 2
HALO = 3
KSIZE = 7
TAPS = KSIZE * KSIZE
ROWS = 8
CONV_ROWS = 16
FCHUNK = 256
CELLS = 256
STEP_ROWS = 16
VMEM_MIB = 58

EPSILON = 1e-06
INV_SQRT2 = 0.7071067811865476
INV_SQRT2PI = 0.3989422804014327
LOG2E = 1.4426950408889634

F32 = jnp.float32
BF16 = jnp.bfloat16
NT = (((1,), (1,)), ((), ()))


def shifted(shard, axis, by):
    count = lax.axis_size(axis)
    pairs = [(i, i + by) for i in range(count) if 0 <= i + by < count]
    return lax.ppermute(shard, axis, pairs)


def params(limit_mib, side=False):
    return pltpu.CompilerParams(vmem_limit_bytes=limit_mib << 20)


def spread(rows, chans):
    height = rows.shape[0]
    row = lax.broadcasted_iota(jnp.int32, (height, height * chans), 0)
    lane = lax.broadcasted_iota(jnp.int32, (height, height * chans), 1)
    pick = ((lane >= row * chans) & (lane < (row + 1) * chans)).astype(F32).astype(BF16)
    wide = jnp.dot(rows.astype(F32).T.astype(BF16), pick, preferred_element_type=F32)
    return [wide[:, r * chans : (r + 1) * chans] for r in range(height)]


def bands_kernel(state_ref, mask_ref, out_ref, left, right):
    edge = state_ref.shape[1]
    low = edge - HALO
    upper = mask_ref[0, 0:8].astype(F32).T
    lower = mask_ref[0, edge - 8 :].astype(F32).T
    for q in range(HALO):
        out_ref[0, 0, q] = (state_ref[0, q].astype(F32) * upper[:, q : q + 1]).astype(BF16)
        p = 8 - HALO + q
        out_ref[0, 1, q] = (state_ref[0, low + q].astype(F32) * lower[:, p : p + 1]).astype(BF16)
    left[...] = state_ref[0, :, 0:16].astype(F32).reshape(left.shape)
    right[...] = state_ref[0, :, edge - 16 :].astype(F32).reshape(right.shape)
    for q in range(HALO):
        out_ref[0, 2, q] = (
            left[pl.ds(q, edge, stride=16), :] * mask_ref[0, :, q : q + 1].astype(F32)
        ).astype(BF16)
        out_ref[0, 3, q] = (
            right[pl.ds(16 - HALO + q, edge, stride=16), :]
            * mask_ref[0, :, low + q : low + q + 1].astype(F32)
        ).astype(BF16)


def bands_call(state, mask):
    slots, edge, _, chans = state.shape
    return pl.pallas_call(
        bands_kernel,
        grid=(slots,),
        in_specs=[
            pl.BlockSpec((1, edge, edge, chans), lambda s: (s, 0, 0, 0)),
            pl.BlockSpec((1, edge, edge), lambda s: (s, 0, 0)),
        ],
        out_specs=pl.BlockSpec((1, 4, HALO, edge, chans), lambda s: (s, 0, 0, 0, 0)),
        out_shape=jax.ShapeDtypeStruct((slots, 4, HALO, edge, chans), BF16),
        scratch_shapes=[pltpu.VMEM((edge * 16, chans), F32)] * 2,
        compiler_params=params(VMEM_MIB),
        name="bands",
    )(state, mask)


def tap(weight_ref, index, chans):
    return jnp.broadcast_to(weight_ref[index : index + 1, :], (8, chans))


def conv_rows(padded, weight_ref, row, column, write, chans, flip=False):
    totals = [None] * CONV_ROWS
    for b in range(KSIZE):
        taps = [a * KSIZE + b for a in range(KSIZE)]
        weights = [tap(weight_ref, TAPS - 1 - t if flip else t, chans) for t in taps]
        for r in range(CONV_ROWS + KSIZE - 1):
            cells = padded[row + r, pl.ds(column + b, 8), :]
            for a in range(KSIZE):
                i = r - a
                if 0 <= i < CONV_ROWS:
                    term = cells * weights[a]
                    totals[i] = term if totals[i] is None else totals[i] + term
    for i in range(CONV_ROWS):
        write(i, totals[i])


def zero_margins(padded):
    rows, cols, chans = padded.shape
    padded[0:HALO] = jnp.zeros((HALO, cols, chans), F32)
    padded[rows - HALO :] = jnp.zeros((HALO, cols, chans), F32)

    def body(r, carry):
        padded[r, 0:8] = jnp.zeros((8, chans), F32)
        padded[r, cols - 8 :] = jnp.zeros((8, chans), F32)
        return carry

    lax.fori_loop(HALO, rows - HALO, body, 0)


def fill_masked(padded, state_ref, mask_ref):
    edge, chans = state_ref.shape[1], state_ref.shape[3]

    def body(n, carry):
        slabs = spread(mask_ref[0, pl.ds(pl.multiple_of(n * 8, 8), 8)], chans)
        for r in range(8):
            i = n * 8 + r
            padded[HALO + i, HALO : HALO + edge] = state_ref[0, i].astype(F32) * slabs[r]
        return carry

    lax.fori_loop(0, edge // 8, body, 0, unroll=4)


def conv_tile(padded, weight_ref, out_ref, base):
    height, edge, chans = out_ref.shape[1:]

    def body(n, carry):
        for g in range(edge // 8):

            def write(i, value):
                out_ref[0, n * CONV_ROWS + i, g * 8 : g * 8 + 8] = value

            conv_rows(padded, weight_ref, base + n * CONV_ROWS, g * 8, write, chans)
        return carry

    lax.fori_loop(0, height // CONV_ROWS, body, 0)


def own_conv_kernel(state_ref, mask_ref, weight_ref, out_ref, padded):
    block = pl.program_id(1)

    @pl.when(block == 0)
    def _():
        zero_margins(padded)
        fill_masked(padded, state_ref, mask_ref)

    conv_tile(padded, weight_ref, out_ref, block * out_ref.shape[1])


def padded_shape(edge, chans):
    return (edge + 2 * HALO, edge + 8, chans)


def conv_cost(slots, edge, chans):
    cells = slots * edge * edge * chans
    return pl.CostEstimate(flops=2 * TAPS * cells, bytes_accessed=8 * cells, transcendentals=0)


def own_conv_call(state, mask, weights):
    slots, edge, _, chans = state.shape
    return pl.pallas_call(
        own_conv_kernel,
        grid=(slots, edge // STEP_ROWS),
        in_specs=[
            pl.BlockSpec((1, edge, edge, chans), lambda s, n: (s, 0, 0, 0)),
            pl.BlockSpec((1, edge, edge), lambda s, n: (s, 0, 0)),
            pl.BlockSpec((TAPS, chans), lambda s, n: (0, 0)),
        ],
        out_specs=pl.BlockSpec((1, STEP_ROWS, edge, chans), lambda s, n: (s, n, 0, 0)),
        out_shape=jax.ShapeDtypeStruct((slots, edge, edge, chans), F32),
        scratch_shapes=[pltpu.VMEM(padded_shape(edge, chans), F32)],
        compiler_params=params(VMEM_MIB),
        cost_estimate=conv_cost(slots, edge, chans),
        name="own_conv",
    )(state, mask, weights)


def window_copies(sources, window, sem):
    slots = sources[0].shape[0]
    return [
        pltpu.make_async_copy(source, window.at[pl.ds(k * slots, slots)], sem.at[k])
        for k, source in enumerate(sources)
    ]


def start_window(sources, window, sem):
    for copy in window_copies(sources, window, sem):
        copy.start()


def wait_window(sources, window, sem):
    for copy in window_copies(sources, window, sem):
        copy.wait()


def picked(window, slot_ref, here_ref, tile, direction, which, q):
    band = window[slot_ref[tile, direction], which, q].astype(F32)
    return jnp.where(here_ref[tile, direction] > 0, band, jnp.zeros_like(band))


def fill_rows(north, south, window, slot_ref, here_ref, tile):
    edge = window.shape[3]
    low = edge - HALO
    for q in range(HALO):
        for target, edge_dir, which, left_dir, right_dir in (
            (north, 0, 1, 4, 5),
            (south, 1, 0, 6, 7),
        ):
            target[q, HALO : HALO + edge] = picked(
                window, slot_ref, here_ref, tile, edge_dir, which, q
            )
            target[q, 0:HALO] = picked(window, slot_ref, here_ref, tile, left_dir, which, q)[low:]
            target[q, HALO + edge : HALO + edge + HALO] = picked(
                window, slot_ref, here_ref, tile, right_dir, which, q
            )[0:HALO]


def fill_columns(west, east, window, slot_ref, here_ref, tile):
    edge = window.shape[3]
    for q in range(HALO):
        west[pl.ds(HALO * 16 + q, edge, stride=16), :] = picked(
            window, slot_ref, here_ref, tile, 2, 3, q
        )
        east[pl.ds(HALO * 16 + 8 + HALO + q, edge, stride=16), :] = picked(
            window, slot_ref, here_ref, tile, 3, 2, q
        )


def fill_margins(padded, window, slot_ref, here_ref, tile):
    rows, stride, chans = padded.shape
    edge = window.shape[3]
    fill_rows(padded.at[0:HALO], padded.at[HALO + edge :], window, slot_ref, here_ref, tile)
    flat = padded.reshape(rows * stride, chans)
    for q in range(HALO):
        flat[pl.ds(HALO * stride + q, edge, stride=stride), :] = picked(
            window, slot_ref, here_ref, tile, 2, 3, q
        )
        flat[pl.ds(HALO * stride + HALO + edge + q, edge, stride=stride), :] = picked(
            window, slot_ref, here_ref, tile, 3, 2, q
        )


def clear_margins(north, south, west, east):
    for ref in (north, south, west, east):
        ref[...] = jnp.zeros_like(ref)


def add_columns(west, east, weight_ref, row, target, base, chans):
    edge = target.shape[1]
    for source, first, taps in ((west, 0, range(HALO)), (east, edge - 8, range(HALO + 1, KSIZE))):
        totals = [target[base + i, first : first + 8] for i in range(ROWS)]
        for b in taps:
            weights = [tap(weight_ref, a * KSIZE + b, chans) for a in range(KSIZE)]
            for r in range(ROWS + KSIZE - 1):
                cells = source[pl.ds((row + r) * 16 + b, 8), :]
                for a in range(KSIZE):
                    i = r - a
                    if 0 <= i < ROWS:
                        totals[i] = totals[i] + cells * weights[a]
        for i in range(ROWS):
            target[base + i, first : first + 8] = totals[i]


def add_rows(source, weight_ref, target, upper, chans):
    height, edge = target.shape[0], target.shape[1]
    pairs = []
    for q in range(HALO):
        for a in range(KSIZE):
            i = q - a if upper else HALO + q + height - a
            if 0 <= i < height:
                pairs.append((q, a, i))
    for g in range(edge // 8):
        rows = sorted({i for _, _, i in pairs})
        totals = {i: target[i, g * 8 : g * 8 + 8] for i in rows}
        for b in range(KSIZE):
            for q in range(HALO):
                cells = source[q, pl.ds(g * 8 + b, 8), :]
                for p, a, i in pairs:
                    if p == q:
                        totals[i] = totals[i] + cells * tap(weight_ref, a * KSIZE + b, chans)
        for i in rows:
            target[i, g * 8 : g * 8 + 8] = totals[i]


def window_scratch(slots, edge, chans):
    return [
        pltpu.VMEM(((2 * REACH + 1) * slots, 4, HALO, edge, chans), BF16),
        pltpu.SemaphoreType.DMA((2 * REACH + 1,)),
    ]


def margin_scratch(slots, edge, chans):
    return window_scratch(slots, edge, chans) + [
        pltpu.VMEM((HALO, edge + 8, chans), F32),
        pltpu.VMEM((HALO, edge + 8, chans), F32),
        pltpu.VMEM(((edge + 2 * HALO) * 16, chans), F32),
        pltpu.VMEM(((edge + 2 * HALO) * 16, chans), F32),
    ]


def margin_setup(sources, slot_ref, here_ref, scratch):
    window, sem, north, south, west, east = scratch
    tile, block = pl.program_id(0), pl.program_id(1)

    @pl.when((tile == 0) & (block == 0))
    def _():
        clear_margins(north, south, west, east)
        wait_window(sources, window, sem)

    @pl.when(block == 0)
    def _():
        fill_rows(north, south, window, slot_ref, here_ref, tile)
        fill_columns(west, east, window, slot_ref, here_ref, tile)


def margin_add(weight_ref, target, scratch, chans):
    _, _, north, south, west, east = scratch
    block, blocks = pl.program_id(1), pl.num_programs(1)
    height = target.shape[0]

    def body(n, carry):
        add_columns(west, east, weight_ref, block * height + n * ROWS, target, n * ROWS, chans)
        return carry

    lax.fori_loop(0, height // ROWS, body, 0, unroll=True)

    @pl.when(block == 0)
    def _():
        add_rows(north, weight_ref, target, True, chans)

    @pl.when(block == blocks - 1)
    def _():
        add_rows(south, weight_ref, target, False, chans)


def folded(values):
    cells, chans = values.shape
    return jnp.sum(values.reshape(cells // 8, 8, chans), 0)


def mlp_cells(parts, par, acc):
    bias, gain, nbias, wup, upb, wdown, dbias, scale, wup_t, wdown_t = par
    gup, gdown, upacc, vec = acc
    units = wup.shape[0]
    chans = wup.shape[1]
    upper = []
    for conv, cot, mask in parts:
        conv = conv + bias[...]
        centred = conv - jnp.mean(conv, axis=-1, keepdims=True)
        inv_std = lax.rsqrt(jnp.mean(centred * centred, axis=-1, keepdims=True) + EPSILON)
        normal = centred * inv_std
        hidden = (normal * gain[...] + nbias[...]).astype(BF16)
        cotm = cot * mask
        dbranch = cotm * scale[...]
        upper.append((normal, inv_std, hidden, cotm, dbranch, dbranch.astype(BF16)))
    acts, dpres = [], []
    for f in range(0, units, FCHUNK):
        part = slice(f, f + FCHUNK)
        total = upacc[part]
        for _, _, hidden, _, _, dbranch_b in upper:
            cells = hidden.shape[0]
            pre = lax.dot_general(wup[part], hidden, NT, preferred_element_type=F32)
            pre = pre + jnp.concatenate([upb[part]] * (cells // 128), 1)
            dact = lax.dot_general(wdown[part], dbranch_b, NT, preferred_element_type=F32)
            cumul = 0.5 + 0.5 * lax.erf(pre * INV_SQRT2)
            slope = cumul + pre * (jnp.exp(-0.5 * pre * pre) * INV_SQRT2PI)
            dpre = dact * slope
            acts.append((pre * cumul).astype(BF16))
            dpres.append(dpre.astype(BF16))
            for lane in range(0, cells, 128):
                total = total + dpre[:, lane : lane + 128]
        upacc[part] = total
    count = len(parts)
    results = []
    sums = [vec[k] for k in range(5)]
    ups, downs = [], []
    for h, (normal, inv_std, hidden, cotm, dbranch, dbranch_b) in enumerate(upper):
        act = jnp.concatenate(acts[h::count], 0)
        dpre_b = jnp.concatenate(dpres[h::count], 0)
        ups.append(jnp.dot(dpre_b, hidden, preferred_element_type=F32))
        downs.append(jnp.dot(act, dbranch_b, preferred_element_type=F32))
        branch = jnp.dot(wdown_t[...], act, preferred_element_type=F32).T + dbias[...]
        dhidden = jnp.dot(wup_t[...], dpre_b, preferred_element_type=F32).T
        dnormal = dhidden * gain[...]
        dconv = inv_std * (
            dnormal
            - jnp.mean(dnormal, axis=-1, keepdims=True)
            - normal * jnp.mean(dnormal * normal, axis=-1, keepdims=True)
        )
        for k, values in enumerate((dconv, dhidden * normal, dhidden, dbranch, cotm * branch)):
            sums[k] = sums[k] + folded(values)
        results.append((branch, dconv))
    gup[...] += sum(ups[1:], ups[0])
    gdown[...] += sum(downs[1:], downs[0])
    for k in range(5):
        vec[k] = sums[k]
    return results


def mlp_kernel(slot_ref, here_ref, *refs):
    sources = refs[:5]
    conv_ref, state_ref, cot_ref, mask_ref, weight_ref = refs[5:10]
    bias, gain, nbias, wup, upb, wdown, dbias, scale = refs[10:18]
    out_ref, grad_ref, bands_ref, gup, gdown, upacc, vec = refs[18:25]
    conv_s, tile_grad, wup_t, wdown_t, upb_s = refs[25:30]
    scratch = refs[30:]
    par = (bias, gain, nbias, wup, upb_s, wdown, dbias, scale, wup_t, wdown_t)
    tile, block, blocks = pl.program_id(0), pl.program_id(1), pl.num_programs(1)
    height, edge, chans = conv_s.shape
    low = edge - HALO

    @pl.when((tile == 0) & (block == 0))
    def _():
        start_window(sources, scratch[0], scratch[1])
        for ref in (gup, gdown, upacc, vec):
            ref[...] = jnp.zeros_like(ref)
        wup_t[...] = wup[...].astype(F32).T.astype(BF16)
        wdown_t[...] = wdown[...].astype(F32).T.astype(BF16)
        upb_s[...] = jnp.broadcast_to(upb[...], (128, upb.shape[1])).T

    margin_setup(sources, slot_ref, here_ref, scratch)
    conv_s[...] = conv_ref[0]
    margin_add(weight_ref, conv_s, scratch, chans)
    rows = CELLS // edge

    def body(n, carry):
        slabs = spread(mask_ref[0, pl.ds(pl.multiple_of(n * ROWS, ROWS), ROWS)], chans)
        parts, places, masks = [], [], []
        for h in range(ROWS // rows):
            first = n * ROWS + h * rows
            place = pl.ds(first, rows)
            mask = jnp.concatenate(slabs[h * rows : (h + 1) * rows], 0)
            places.append((first, place))
            masks.append(mask)
            parts.append(
                (
                    conv_s[place].reshape(CELLS, chans),
                    cot_ref[0, place].astype(F32).reshape(CELLS, chans),
                    mask,
                )
            )
        results = mlp_cells(parts, par, (gup, gdown, upacc, vec))
        for (first, place), mask, (branch, dconv) in zip(places, masks, results):
            state = state_ref[0, place].astype(F32).reshape(CELLS, chans)
            output = (state + (mask * scale[...]) * branch).astype(BF16)
            out_ref[0, place] = output.reshape(rows, edge, chans)
            grad_ref[0, place] = dconv.reshape(rows, edge, chans)
            start = pl.multiple_of((block * height + first) * edge, CELLS)
            tile_grad[pl.ds(start, CELLS), :] = dconv
        return carry

    lax.fori_loop(0, height // ROWS, body, 0, unroll=True)

    @pl.when(block == blocks - 1)
    def _():
        for q in range(HALO):
            bands_ref[0, 0, q] = tile_grad[q * edge : (q + 1) * edge].astype(BF16)
            bands_ref[0, 1, q] = tile_grad[(low + q) * edge : (low + q + 1) * edge].astype(BF16)
            bands_ref[0, 2, q] = tile_grad[pl.ds(q, edge, stride=edge), :].astype(BF16)
            bands_ref[0, 3, q] = tile_grad[pl.ds(low + q, edge, stride=edge), :].astype(BF16)


def mlp_call(slot, here, sources, conv, state, cot, mask, weights, par):
    slots, edge, _, chans = state.shape
    units = par[3].shape[0]
    blocks = edge // STEP_ROWS
    row_spec = pl.BlockSpec((1, STEP_ROWS, edge, chans), lambda s, n, *_: (s, n, 0, 0))

    def whole(a):
        return pl.BlockSpec(a.shape, lambda s, n, *_: (0,) * a.ndim)

    grid_spec = pltpu.PrefetchScalarGridSpec(
        num_scalar_prefetch=2,
        grid=(slots, blocks),
        in_specs=[pl.BlockSpec(memory_space=pl.ANY)] * 5
        + [
            row_spec,
            row_spec,
            row_spec,
            pl.BlockSpec((1, STEP_ROWS, edge), lambda s, n, *_: (s, n, 0)),
            whole(weights),
        ]
        + [whole(a) for a in par],
        out_specs=[
            row_spec,
            row_spec,
            pl.BlockSpec((1, 4, HALO, edge, chans), lambda s, n, *_: (s, 0, 0, 0, 0)),
            pl.BlockSpec((units, chans), lambda s, n, *_: (0, 0)),
            pl.BlockSpec((units, chans), lambda s, n, *_: (0, 0)),
            pl.BlockSpec((units, 128), lambda s, n, *_: (0, 0)),
            pl.BlockSpec((5, 8, chans), lambda s, n, *_: (0, 0, 0)),
        ],
        scratch_shapes=[
            pltpu.VMEM((STEP_ROWS, edge, chans), F32),
            pltpu.VMEM((edge * edge, chans), F32),
            pltpu.VMEM((chans, units), BF16),
            pltpu.VMEM((chans, units), BF16),
            pltpu.VMEM((units, 128), F32),
        ]
        + margin_scratch(slots, edge, chans),
    )
    cells = slots * edge * edge
    return pl.pallas_call(
        mlp_kernel,
        grid_spec=grid_spec,
        out_shape=[
            jax.ShapeDtypeStruct(state.shape, BF16),
            jax.ShapeDtypeStruct(state.shape, F32),
            jax.ShapeDtypeStruct((slots, 4, HALO, edge, chans), BF16),
            jax.ShapeDtypeStruct((units, chans), F32),
            jax.ShapeDtypeStruct((units, chans), F32),
            jax.ShapeDtypeStruct((units, 128), F32),
            jax.ShapeDtypeStruct((5, 8, chans), F32),
        ],
        compiler_params=params(VMEM_MIB),
        cost_estimate=pl.CostEstimate(
            flops=12 * cells * units * chans, bytes_accessed=14 * cells * chans, transcendentals=0
        ),
        name="mlp",
    )(slot, here, *sources, conv, state, cot, mask, weights, *par)


def tap_grad_kernel(slot_ref, here_ref, *refs):
    sources = refs[:5]
    state_ref, mask_ref, grad_ref, gup, gdown, upacc, vec, out_ref = refs[5:13]
    padded, totals, small = refs[13:16]
    window, sem = refs[16:]
    tile, tiles = pl.program_id(0), pl.num_programs(0)
    edge, chans = grad_ref.shape[1], grad_ref.shape[3]

    @pl.when(tile == 0)
    def _():
        start_window(sources, window, sem)
        totals[...] = jnp.zeros_like(totals)
        zero_margins(padded)

    fill_masked(padded, state_ref, mask_ref)

    @pl.when(tile == 0)
    def _():
        wait_window(sources, window, sem)

    fill_margins(padded, window, slot_ref, here_ref, tile)

    for b in range(KSIZE):

        def body(n, sums, b=b):
            sums = list(sums)
            row = n * ROWS
            for g in range(edge // 8):
                grads = [grad_ref[0, row + i, g * 8 : g * 8 + 8] for i in range(ROWS)]
                for r in range(ROWS + KSIZE - 1):
                    cells = padded[row + r, pl.ds(g * 8 + b, 8), :]
                    for a in range(KSIZE):
                        if 0 <= r - a < ROWS:
                            sums[a] = sums[a] + cells * grads[r - a]
            return tuple(sums)

        start = tuple(totals[a * KSIZE + b] for a in range(KSIZE))
        sums = lax.fori_loop(0, edge // ROWS, body, start)
        for a in range(KSIZE):
            totals[a * KSIZE + b] = sums[a]

    @pl.when(tile == tiles - 1)
    def _():
        small[...] = jnp.zeros_like(small)
        small[0:TAPS] = jnp.sum(totals[...], 1)
        small[TAPS : TAPS + 5] = jnp.sum(vec[...], 1)
        units = upacc.shape[0]
        for u in range(units // 128):
            small[TAPS + 5 + u : TAPS + 6 + u] = jnp.sum(
                upacc[u * 128 : (u + 1) * 128].T, 0, keepdims=True
            )
        high = small[...].astype(BF16)
        rest = (small[...] - high.astype(F32)).astype(BF16)
        count, rows = out_ref.shape[0], small.shape[0]
        share = units // count
        for d in range(count):
            part = slice(d * share, (d + 1) * share)
            out_ref[d, 0:share] = gup[part].astype(BF16)
            out_ref[d, share : 2 * share] = gdown[part].astype(BF16)
            out_ref[d, 2 * share : 2 * share + rows] = high
            out_ref[d, 2 * share + rows :] = rest


def tap_grad_call(slot, here, sources, state, mask, grad, gup, gdown, upacc, vec, count):
    slots, edge, _, chans = state.shape
    rows = TAPS + 5 + upacc.shape[0] // 128
    rows = -(-rows // 16) * 16
    length = 2 * (upacc.shape[0] // count) + 2 * rows
    tile_spec = pl.BlockSpec((1, edge, edge, chans), lambda s, *_: (s, 0, 0, 0))
    grid_spec = pltpu.PrefetchScalarGridSpec(
        num_scalar_prefetch=2,
        grid=(slots,),
        in_specs=[pl.BlockSpec(memory_space=pl.ANY)] * 5
        + [
            tile_spec,
            pl.BlockSpec((1, edge, edge), lambda s, *_: (s, 0, 0)),
            tile_spec,
            pl.BlockSpec(gup.shape, lambda s, *_: (0, 0)),
            pl.BlockSpec(gdown.shape, lambda s, *_: (0, 0)),
            pl.BlockSpec(upacc.shape, lambda s, *_: (0, 0)),
            pl.BlockSpec(vec.shape, lambda s, *_: (0, 0, 0)),
        ],
        out_specs=pl.BlockSpec((count, length, chans), lambda s, *_: (0, 0, 0)),
        scratch_shapes=[
            pltpu.VMEM(padded_shape(edge, chans), F32),
            pltpu.VMEM((TAPS, 8, chans), F32),
            pltpu.VMEM((rows, chans), F32),
        ]
        + window_scratch(slots, edge, chans),
    )
    return pl.pallas_call(
        tap_grad_kernel,
        grid_spec=grid_spec,
        out_shape=jax.ShapeDtypeStruct((count, length, chans), BF16),
        compiler_params=params(VMEM_MIB),
        cost_estimate=conv_cost(slots, edge, chans),
        name="tap_grad",
    )(slot, here, *sources, state, mask, grad, gup, gdown, upacc, vec)


def state_grad_kernel(slot_ref, here_ref, *refs):
    sources = refs[:5]
    grad_ref, cot_ref, mask_ref, weight_ref, out_ref, padded, conv_s, window, sem = refs[5:]
    tile = pl.program_id(0)
    edge, chans = grad_ref.shape[1], grad_ref.shape[3]

    @pl.when(tile == 0)
    def _():
        start_window(sources, window, sem)
        zero_margins(padded)

    def fill(n, carry):
        for r in range(8):
            i = n * 8 + r
            padded[HALO + i, HALO : HALO + edge] = grad_ref[0, i]
        return carry

    lax.fori_loop(0, edge // 8, fill, 0)

    @pl.when(tile == 0)
    def _():
        wait_window(sources, window, sem)

    fill_margins(padded, window, slot_ref, here_ref, tile)

    def body(n, carry):
        row = n * CONV_ROWS
        for g in range(edge // 8):

            def write(i, value):
                conv_s[i, g * 8 : g * 8 + 8] = value

            conv_rows(padded, weight_ref, row, g * 8, write, chans, True)
        for k in range(0, CONV_ROWS, 8):
            slabs = spread(mask_ref[0, pl.ds(pl.multiple_of(row + k, 8), 8)], chans)
            for r in range(8):
                i = row + k + r
                out_ref[0, i] = (cot_ref[0, i].astype(F32) + slabs[r] * conv_s[k + r]).astype(BF16)
        return carry

    lax.fori_loop(0, edge // CONV_ROWS, body, 0)


def state_grad_call(slot, here, sources, grad, cot, mask, weights):
    slots, edge, _, chans = cot.shape
    tile_spec = pl.BlockSpec((1, edge, edge, chans), lambda s, *_: (s, 0, 0, 0))
    grid_spec = pltpu.PrefetchScalarGridSpec(
        num_scalar_prefetch=2,
        grid=(slots,),
        in_specs=[pl.BlockSpec(memory_space=pl.ANY)] * 5
        + [
            tile_spec,
            tile_spec,
            pl.BlockSpec((1, edge, edge), lambda s, *_: (s, 0, 0)),
            pl.BlockSpec((TAPS, chans), lambda s, *_: (0, 0)),
        ],
        out_specs=tile_spec,
        scratch_shapes=[
            pltpu.VMEM(padded_shape(edge, chans), F32),
            pltpu.VMEM((CONV_ROWS, edge, chans), F32),
        ]
        + window_scratch(slots, edge, chans),
    )
    return pl.pallas_call(
        state_grad_kernel,
        grid_spec=grid_spec,
        out_shape=jax.ShapeDtypeStruct(cot.shape, BF16),
        compiler_params=params(VMEM_MIB),
        cost_estimate=conv_cost(slots, edge, chans),
        name="state_grad",
    )(slot, here, *sources, grad, cot, mask, weights)


def total_kernel(pieces_ref, up_ref, down_ref, taps_ref, vec_ref, bias_ref):
    share = up_ref.shape[0]
    rows = (pieces_ref.shape[1] - 2 * share) // 2
    total = pieces_ref[0].astype(F32)
    for d in range(1, pieces_ref.shape[0]):
        total = total + pieces_ref[d].astype(F32)
    up_ref[...] = total[:share]
    down_ref[...] = total[share : 2 * share]
    small = total[2 * share : 2 * share + rows] + total[2 * share + rows :]
    taps_ref[...] = small[:TAPS]
    vec_ref[...] = small[TAPS : TAPS + 5]
    bias_ref[...] = small[TAPS + 5 : TAPS + 5 + bias_ref.shape[0]]


def total_call(pieces, units):
    count, _, chans = pieces.shape
    share = units // count
    shapes = [(share, chans), (share, chans), (TAPS, chans), (5, chans), (units // chans, chans)]
    return pl.pallas_call(
        total_kernel,
        out_shape=[jax.ShapeDtypeStruct(shape, F32) for shape in shapes],
        compiler_params=params(VMEM_MIB),
        name="total",
    )(pieces)


def pair_pairs():
    return [(i, i ^ 1) for i in range(lax.axis_size("tx"))]


def direct(bands):
    return (
        shifted(bands, "tx", 2),
        lax.ppermute(bands, "tx", pair_pairs()),
        shifted(bands, "tx", -2),
    )


def relayed(below, above):
    odd = lax.axis_index("tx") % 2 == 1
    return lax.ppermute(jnp.where(odd, below, above), "tx", pair_pairs())


def window_slots(neighbours, slots):
    me = lax.axis_index("tx")
    low = (me - REACH) * slots
    slot = jnp.clip(neighbours - low, 0, (2 * REACH + 1) * slots - 1)
    swap = (me % 2 == 1) & ((slot // slots == 1) | (slot // slots == 3))
    return jnp.where(swap, slot + jnp.where(slot // slots == 1, 2, -2) * slots, slot)


def per_device(
    tile_state,
    cotangent,
    neighbours,
    land_mask,
    kernel,
    conv_bias,
    norm_gain,
    norm_bias,
    w_up,
    up_bias,
    w_down,
    down_bias,
    layer_scale,
):
    slots, edge, chans = (tile_state.shape[0], tile_state.shape[1], tile_state.shape[3])
    units = w_up.shape[0]
    count = lax.axis_size("tx")
    mask = land_mask.reshape(slots, edge, edge)
    here = (neighbours >= 0).astype(jnp.int32)
    slot = window_slots(neighbours, slots)
    par = (
        conv_bias[None],
        norm_gain[None],
        norm_bias[None],
        w_up,
        up_bias[None],
        w_down,
        down_bias[None],
        layer_scale[None],
    )

    bands = bands_call(tile_state, mask)
    below, partner, above = direct(bands)
    window = [below, relayed(below, above), bands, partner, above]
    conv = own_conv_call(tile_state, mask, kernel)
    block_out, grad, grad_bands, gup, gdown, upacc, vec = mlp_call(
        slot, here, window, conv, tile_state, cotangent, mask, kernel, par
    )
    below, partner, above = direct(grad_bands)

    pieces = tap_grad_call(
        slot, here, window, tile_state, mask, grad, gup, gdown, upacc, vec, count
    )
    pieces, below, above, grad = lax.optimization_barrier((pieces, below, above, grad))
    relay = relayed(below, above)
    pieces, relay, grad = lax.optimization_barrier((pieces, relay, grad))
    grad_window = [below, relay, grad_bands, partner, above]
    pieces = lax.all_to_all(pieces, "tx", 0, 0, tiled=True)
    grad_state = state_grad_call(slot, here, grad_window, grad, cotangent, mask, kernel)

    grad_up, grad_down, grad_kernel, grad_vectors, grad_up_bias = total_call(pieces, units)
    grad_up_bias = grad_up_bias.reshape(units)
    return (block_out, grad_state, grad_up, grad_down, grad_kernel, grad_vectors, grad_up_bias)


def solution(mesh):
    tiles = P(("groups", "tx"), None, None, None)
    rows = P(("groups", "tx"), None)
    return jax.shard_map(
        per_device,
        mesh=mesh,
        in_specs=(tiles, tiles, rows, rows) + (P(),) * 9,
        out_specs=(tiles, tiles, rows, rows, P("groups", None), P("groups", None), P("groups")),
        check_vma=False,
    )
```

```python
import functools

import jax
import jax.numpy as jnp
from jax import lax
from jax.experimental import pallas as pl
from jax.experimental.pallas import tpu as pltpu
from jax.sharding import PartitionSpec as P

REACH = 2
HALO = 3
KSIZE = 7
TAPS = KSIZE * KSIZE
ROWS = 8
CONV_ROWS = 16
FCHUNK = 256
CELLS = 256
STEP_ROWS = 16
TAP_ROWS = 32
VMEM_MIB = 58

EPSILON = 1e-06
INV_SQRT2 = 0.7071067811865476
INV_SQRT2PI = 0.3989422804014327
LOG2E = 1.4426950408889634

F32 = jnp.float32
BF16 = jnp.bfloat16
NT = (((1,), (1,)), ((), ()))


def shifted(shard, axis, by):
    count = lax.axis_size(axis)
    pairs = [(i, i + by) for i in range(count) if 0 <= i + by < count]
    return lax.ppermute(shard, axis, pairs)


def params(limit_mib, side=False):
    return pltpu.CompilerParams(vmem_limit_bytes=limit_mib << 20)


def spread(rows, chans):
    height = rows.shape[0]
    row = lax.broadcasted_iota(jnp.int32, (height, height * chans), 0)
    lane = lax.broadcasted_iota(jnp.int32, (height, height * chans), 1)
    pick = ((lane >= row * chans) & (lane < (row + 1) * chans)).astype(F32).astype(BF16)
    wide = jnp.dot(rows.astype(F32).T.astype(BF16), pick, preferred_element_type=F32)
    return [wide[:, r * chans : (r + 1) * chans] for r in range(height)]


def bands_kernel(top_ref, low_ref, left_ref, right_ref, mask_ref, out_ref, left, right):
    edge = mask_ref.shape[1]
    low = edge - HALO
    upper = mask_ref[0, 0:8].astype(F32).T
    lower = mask_ref[0, edge - 8 :].astype(F32).T
    for q in range(HALO):
        out_ref[0, 0, q] = (top_ref[0, q].astype(F32) * upper[:, q : q + 1]).astype(BF16)
        p = 8 - HALO + q
        out_ref[0, 1, q] = (low_ref[0, p].astype(F32) * lower[:, p : p + 1]).astype(BF16)
    left[...] = left_ref[0].astype(F32).reshape(left.shape)
    right[...] = right_ref[0].astype(F32).reshape(right.shape)
    for q in range(HALO):
        out_ref[0, 2, q] = (
            left[pl.ds(q, edge, stride=16), :] * mask_ref[0, :, q : q + 1].astype(F32)
        ).astype(BF16)
        out_ref[0, 3, q] = (
            right[pl.ds(16 - HALO + q, edge, stride=16), :]
            * mask_ref[0, :, low + q : low + q + 1].astype(F32)
        ).astype(BF16)


def bands_call(state, mask):
    slots, edge, _, chans = state.shape
    return pl.pallas_call(
        bands_kernel,
        grid=(slots,),
        in_specs=[
            pl.BlockSpec((1, 8, edge, chans), lambda s: (s, 0, 0, 0)),
            pl.BlockSpec((1, 8, edge, chans), lambda s: (s, edge // 8 - 1, 0, 0)),
            pl.BlockSpec((1, edge, 16, chans), lambda s: (s, 0, 0, 0)),
            pl.BlockSpec((1, edge, 16, chans), lambda s: (s, 0, edge // 16 - 1, 0)),
            pl.BlockSpec((1, edge, edge), lambda s: (s, 0, 0)),
        ],
        out_specs=pl.BlockSpec((1, 4, HALO, edge, chans), lambda s: (s, 0, 0, 0, 0)),
        out_shape=jax.ShapeDtypeStruct((slots, 4, HALO, edge, chans), BF16),
        scratch_shapes=[pltpu.VMEM((edge * 16, chans), F32)] * 2,
        compiler_params=params(VMEM_MIB),
        name="bands",
    )(state, state, state, state, mask)


def tap(weight_ref, index, chans):
    return jnp.broadcast_to(weight_ref[index : index + 1, :], (8, chans))


def conv_rows(padded, weight_ref, row, column, write, chans, flip=False):
    totals = [None] * CONV_ROWS
    for b in range(KSIZE):
        taps = [a * KSIZE + b for a in range(KSIZE)]
        weights = [tap(weight_ref, TAPS - 1 - t if flip else t, chans) for t in taps]
        for r in range(CONV_ROWS + KSIZE - 1):
            cells = padded[row + r, pl.ds(column + b, 8), :]
            for a in range(KSIZE):
                i = r - a
                if 0 <= i < CONV_ROWS:
                    term = cells * weights[a]
                    totals[i] = term if totals[i] is None else totals[i] + term
    for i in range(CONV_ROWS):
        write(i, totals[i])


def zero_margins(padded):
    rows, cols, chans = padded.shape
    padded[0:HALO] = jnp.zeros((HALO, cols, chans), F32)
    padded[rows - HALO :] = jnp.zeros((HALO, cols, chans), F32)

    def body(r, carry):
        padded[r, 0:8] = jnp.zeros((8, chans), F32)
        padded[r, cols - 8 :] = jnp.zeros((8, chans), F32)
        return carry

    lax.fori_loop(HALO, rows - HALO, body, 0)


def fill_masked(padded, state_ref, mask_ref):
    edge, chans = state_ref.shape[1], state_ref.shape[3]

    def body(n, carry):
        slabs = spread(mask_ref[0, pl.ds(pl.multiple_of(n * 8, 8), 8)], chans)
        for r in range(8):
            i = n * 8 + r
            padded[HALO + i, HALO : HALO + edge] = state_ref[0, i].astype(F32) * slabs[r]
        return carry

    lax.fori_loop(0, edge // 8, body, 0, unroll=4)


def conv_tile(padded, weight_ref, out_ref, base):
    height, edge, chans = out_ref.shape[1:]

    def body(n, carry):
        for g in range(edge // 8):

            def write(i, value):
                out_ref[0, n * CONV_ROWS + i, g * 8 : g * 8 + 8] = value

            conv_rows(padded, weight_ref, base + n * CONV_ROWS, g * 8, write, chans)
        return carry

    lax.fori_loop(0, height // CONV_ROWS, body, 0)


def own_conv_kernel(state_ref, mask_ref, weight_ref, out_ref, padded):
    block = pl.program_id(1)

    @pl.when(block == 0)
    def _():
        zero_margins(padded)
        fill_masked(padded, state_ref, mask_ref)

    conv_tile(padded, weight_ref, out_ref, block * out_ref.shape[1])


def padded_shape(edge, chans):
    return (edge + 2 * HALO, edge + 8, chans)


def conv_cost(slots, edge, chans):
    cells = slots * edge * edge * chans
    return pl.CostEstimate(flops=2 * TAPS * cells, bytes_accessed=8 * cells, transcendentals=0)


def own_conv_call(state, mask, weights):
    slots, edge, _, chans = state.shape
    return pl.pallas_call(
        own_conv_kernel,
        grid=(slots, edge // STEP_ROWS),
        in_specs=[
            pl.BlockSpec((1, edge, edge, chans), lambda s, n: (s, 0, 0, 0)),
            pl.BlockSpec((1, edge, edge), lambda s, n: (s, 0, 0)),
            pl.BlockSpec((TAPS, chans), lambda s, n: (0, 0)),
        ],
        out_specs=pl.BlockSpec((1, STEP_ROWS, edge, chans), lambda s, n: (s, n, 0, 0)),
        out_shape=jax.ShapeDtypeStruct((slots, edge, edge, chans), F32),
        scratch_shapes=[pltpu.VMEM(padded_shape(edge, chans), F32)],
        compiler_params=params(VMEM_MIB),
        cost_estimate=conv_cost(slots, edge, chans),
        name="own_conv",
    )(state, mask, weights)


def window_copies(sources, window, sem):
    slots = sources[0].shape[0]
    return [
        pltpu.make_async_copy(source, window.at[pl.ds(k * slots, slots)], sem.at[k])
        for k, source in enumerate(sources)
    ]


def start_window(sources, window, sem):
    for copy in window_copies(sources, window, sem):
        copy.start()


def wait_window(sources, window, sem):
    for copy in window_copies(sources, window, sem):
        copy.wait()


def picked(window, table_ref, me_ref, tile, direction, which, q):
    slots = window.shape[0] // (2 * REACH + 1)
    me, entry = me_ref[0], table_ref[tile, direction]
    slot = jnp.clip(entry - (me - REACH) * slots, 0, (2 * REACH + 1) * slots - 1)
    place = lax.div(slot, slots)
    odd = lax.rem(me, 2) == 1
    shift = jnp.where(place == 1, 2 * slots, jnp.where(place == 3, -2 * slots, 0))
    slot = slot + jnp.where(odd, shift, 0)
    band = window[slot, which, q].astype(F32)
    return jnp.where(entry >= 0, band, jnp.zeros_like(band))


def fill_rows(north, south, window, table_ref, me_ref, tile):
    edge = window.shape[3]
    low = edge - HALO
    for q in range(HALO):
        for target, edge_dir, which, left_dir, right_dir in (
            (north, 0, 1, 4, 5),
            (south, 1, 0, 6, 7),
        ):
            target[q, HALO : HALO + edge] = picked(
                window, table_ref, me_ref, tile, edge_dir, which, q
            )
            target[q, 0:HALO] = picked(window, table_ref, me_ref, tile, left_dir, which, q)[low:]
            target[q, HALO + edge : HALO + edge + HALO] = picked(
                window, table_ref, me_ref, tile, right_dir, which, q
            )[0:HALO]


def fill_columns(west, east, window, table_ref, me_ref, tile):
    edge = window.shape[3]
    for q in range(HALO):
        west[pl.ds(HALO * 16 + q, edge, stride=16), :] = picked(
            window, table_ref, me_ref, tile, 2, 3, q
        )
        east[pl.ds(HALO * 16 + 8 + HALO + q, edge, stride=16), :] = picked(
            window, table_ref, me_ref, tile, 3, 2, q
        )


def fill_margins(padded, window, table_ref, me_ref, tile):
    rows, stride, chans = padded.shape
    edge = window.shape[3]
    fill_rows(padded.at[0:HALO], padded.at[HALO + edge :], window, table_ref, me_ref, tile)
    flat = padded.reshape(rows * stride, chans)
    for q in range(HALO):
        flat[pl.ds(HALO * stride + q, edge, stride=stride), :] = picked(
            window, table_ref, me_ref, tile, 2, 3, q
        )
        flat[pl.ds(HALO * stride + HALO + edge + q, edge, stride=stride), :] = picked(
            window, table_ref, me_ref, tile, 3, 2, q
        )


def clear_margins(north, south, west, east):
    for ref in (north, south, west, east):
        ref[...] = jnp.zeros_like(ref)


def add_columns(west, east, weight_ref, row, target, base, chans):
    edge = target.shape[1]
    for source, first, taps in ((west, 0, range(HALO)), (east, edge - 8, range(HALO + 1, KSIZE))):
        totals = [target[base + i, first : first + 8] for i in range(ROWS)]
        for b in taps:
            weights = [tap(weight_ref, a * KSIZE + b, chans) for a in range(KSIZE)]
            for r in range(ROWS + KSIZE - 1):
                cells = source[pl.ds((row + r) * 16 + b, 8), :]
                for a in range(KSIZE):
                    i = r - a
                    if 0 <= i < ROWS:
                        totals[i] = totals[i] + cells * weights[a]
        for i in range(ROWS):
            target[base + i, first : first + 8] = totals[i]


def add_rows(source, weight_ref, target, upper, chans):
    height, edge = target.shape[0], target.shape[1]
    pairs = []
    for q in range(HALO):
        for a in range(KSIZE):
            i = q - a if upper else HALO + q + height - a
            if 0 <= i < height:
                pairs.append((q, a, i))
    for g in range(edge // 8):
        rows = sorted({i for _, _, i in pairs})
        totals = {i: target[i, g * 8 : g * 8 + 8] for i in rows}
        for b in range(KSIZE):
            for q in range(HALO):
                cells = source[q, pl.ds(g * 8 + b, 8), :]
                for p, a, i in pairs:
                    if p == q:
                        totals[i] = totals[i] + cells * tap(weight_ref, a * KSIZE + b, chans)
        for i in rows:
            target[i, g * 8 : g * 8 + 8] = totals[i]


def window_scratch(slots, edge, chans):
    return [
        pltpu.VMEM(((2 * REACH + 1) * slots, 4, HALO, edge, chans), BF16),
        pltpu.SemaphoreType.DMA((2 * REACH + 1,)),
    ]


def margin_scratch(slots, edge, chans):
    return window_scratch(slots, edge, chans) + [
        pltpu.VMEM((HALO, edge + 8, chans), F32),
        pltpu.VMEM((HALO, edge + 8, chans), F32),
        pltpu.VMEM(((edge + 2 * HALO) * 16, chans), F32),
        pltpu.VMEM(((edge + 2 * HALO) * 16, chans), F32),
    ]


def margin_setup(sources, table_ref, me_ref, scratch):
    window, sem, north, south, west, east = scratch
    tile, block = pl.program_id(0), pl.program_id(1)

    @pl.when((tile == 0) & (block == 0))
    def _():
        clear_margins(north, south, west, east)
        wait_window(sources, window, sem)

    @pl.when(block == 0)
    def _():
        fill_rows(north, south, window, table_ref, me_ref, tile)
        fill_columns(west, east, window, table_ref, me_ref, tile)


def margin_add(weight_ref, target, scratch, chans):
    _, _, north, south, west, east = scratch
    block, blocks = pl.program_id(1), pl.num_programs(1)
    height = target.shape[0]

    def body(n, carry):
        add_columns(west, east, weight_ref, block * height + n * ROWS, target, n * ROWS, chans)
        return carry

    lax.fori_loop(0, height // ROWS, body, 0, unroll=True)

    @pl.when(block == 0)
    def _():
        add_rows(north, weight_ref, target, True, chans)

    @pl.when(block == blocks - 1)
    def _():
        add_rows(south, weight_ref, target, False, chans)


def folded(values):
    cells, chans = values.shape
    return jnp.sum(values.reshape(cells // 8, 8, chans), 0)


def mlp_cells(parts, par, acc):
    bias, gain, nbias, wup, upb, wdown, dbias, scale, wup_t, wdown_t = par
    gup, gdown, upacc, vec = acc
    units = wup.shape[0]
    chans = wup.shape[1]
    upper = []
    for conv, cot, mask in parts:
        conv = conv + bias[...]
        centred = conv - jnp.mean(conv, axis=-1, keepdims=True)
        inv_std = lax.rsqrt(jnp.mean(centred * centred, axis=-1, keepdims=True) + EPSILON)
        normal = centred * inv_std
        hidden = (normal * gain[...] + nbias[...]).astype(BF16)
        cotm = cot * mask
        dbranch = cotm * scale[...]
        upper.append((normal, inv_std, hidden, cotm, dbranch, dbranch.astype(BF16)))
    acts, dpres = [], []
    for f in range(0, units, FCHUNK):
        part = slice(f, f + FCHUNK)
        total = upacc[part]
        for _, _, hidden, _, _, dbranch_b in upper:
            cells = hidden.shape[0]
            pre = lax.dot_general(wup[part], hidden, NT, preferred_element_type=F32)
            pre = pre + jnp.concatenate([upb[part]] * (cells // 128), 1)
            dact = lax.dot_general(wdown[part], dbranch_b, NT, preferred_element_type=F32)
            cumul = 0.5 + 0.5 * lax.erf(pre * INV_SQRT2)
            slope = cumul + pre * (jnp.exp(-0.5 * pre * pre) * INV_SQRT2PI)
            dpre = dact * slope
            acts.append((pre * cumul).astype(BF16))
            dpres.append(dpre.astype(BF16))
            for lane in range(0, cells, 128):
                total = total + dpre[:, lane : lane + 128]
        upacc[part] = total
    count = len(parts)
    results = []
    sums = [vec[k] for k in range(5)]
    ups, downs = [], []
    for h, (normal, inv_std, hidden, cotm, dbranch, dbranch_b) in enumerate(upper):
        act = jnp.concatenate(acts[h::count], 0)
        dpre_b = jnp.concatenate(dpres[h::count], 0)
        ups.append(jnp.dot(dpre_b, hidden, preferred_element_type=F32))
        downs.append(jnp.dot(act, dbranch_b, preferred_element_type=F32))
        branch = jnp.dot(wdown_t[...], act, preferred_element_type=F32).T + dbias[...]
        dhidden = jnp.dot(wup_t[...], dpre_b, preferred_element_type=F32).T
        dnormal = dhidden * gain[...]
        dconv = inv_std * (
            dnormal
            - jnp.mean(dnormal, axis=-1, keepdims=True)
            - normal * jnp.mean(dnormal * normal, axis=-1, keepdims=True)
        )
        for k, values in enumerate((dconv, dhidden * normal, dhidden, dbranch, cotm * branch)):
            sums[k] = sums[k] + folded(values)
        results.append((branch, dconv))
    gup[...] += sum(ups[1:], ups[0])
    gdown[...] += sum(downs[1:], downs[0])
    for k in range(5):
        vec[k] = sums[k]
    return results


def mlp_kernel(table_ref, me_ref, *refs):
    sources = refs[:5]
    conv_ref, state_ref, cot_ref, mask_ref, weight_ref = refs[5:10]
    bias, gain, nbias, wup, upb, wdown, dbias, scale = refs[10:18]
    out_ref, grad_ref, bands_ref, gup, gdown, upacc, vec = refs[18:25]
    conv_s, tile_grad, wup_t, wdown_t, upb_s = refs[25:30]
    scratch = refs[30:]
    par = (bias, gain, nbias, wup, upb_s, wdown, dbias, scale, wup_t, wdown_t)
    tile, block, blocks = pl.program_id(0), pl.program_id(1), pl.num_programs(1)
    height, edge, chans = conv_s.shape
    low = edge - HALO

    @pl.when((tile == 0) & (block == 0))
    def _():
        start_window(sources, scratch[0], scratch[1])
        for ref in (gup, gdown, upacc, vec):
            ref[...] = jnp.zeros_like(ref)
        wup_t[...] = wup[...].astype(F32).T.astype(BF16)
        wdown_t[...] = wdown[...].astype(F32).T.astype(BF16)
        upb_s[...] = jnp.broadcast_to(upb[...], (128, upb.shape[1])).T

    margin_setup(sources, table_ref, me_ref, scratch)
    conv_s[...] = conv_ref[0]
    margin_add(weight_ref, conv_s, scratch, chans)
    rows = CELLS // edge

    def body(n, carry):
        slabs = spread(mask_ref[0, pl.ds(pl.multiple_of(n * ROWS, ROWS), ROWS)], chans)
        parts, places, masks = [], [], []
        for h in range(ROWS // rows):
            first = n * ROWS + h * rows
            place = pl.ds(first, rows)
            mask = jnp.concatenate(slabs[h * rows : (h + 1) * rows], 0)
            places.append((first, place))
            masks.append(mask)
            parts.append(
                (
                    conv_s[place].reshape(CELLS, chans),
                    cot_ref[0, place].astype(F32).reshape(CELLS, chans),
                    mask,
                )
            )
        results = mlp_cells(parts, par, (gup, gdown, upacc, vec))
        for (first, place), mask, (branch, dconv) in zip(places, masks, results):
            state = state_ref[0, place].astype(F32).reshape(CELLS, chans)
            output = (state + (mask * scale[...]) * branch).astype(BF16)
            out_ref[0, place] = output.reshape(rows, edge, chans)
            grad_ref[0, place] = dconv.astype(BF16).reshape(rows, edge, chans)
            start = pl.multiple_of((block * height + first) * edge, CELLS)
            tile_grad[pl.ds(start, CELLS), :] = dconv
        return carry

    lax.fori_loop(0, height // ROWS, body, 0, unroll=True)

    @pl.when(block == blocks - 1)
    def _():
        for q in range(HALO):
            bands_ref[0, 0, q] = tile_grad[q * edge : (q + 1) * edge].astype(BF16)
            bands_ref[0, 1, q] = tile_grad[(low + q) * edge : (low + q + 1) * edge].astype(BF16)
            bands_ref[0, 2, q] = tile_grad[pl.ds(q, edge, stride=edge), :].astype(BF16)
            bands_ref[0, 3, q] = tile_grad[pl.ds(low + q, edge, stride=edge), :].astype(BF16)


def mlp_call(table, me, sources, conv, state, cot, mask, weights, par):
    slots, edge, _, chans = state.shape
    units = par[3].shape[0]
    blocks = edge // STEP_ROWS
    row_spec = pl.BlockSpec((1, STEP_ROWS, edge, chans), lambda s, n, *_: (s, n, 0, 0))

    def whole(a):
        return pl.BlockSpec(a.shape, lambda s, n, *_: (0,) * a.ndim)

    grid_spec = pltpu.PrefetchScalarGridSpec(
        num_scalar_prefetch=2,
        grid=(slots, blocks),
        in_specs=[pl.BlockSpec(memory_space=pl.ANY)] * 5
        + [
            row_spec,
            row_spec,
            row_spec,
            pl.BlockSpec((1, STEP_ROWS, edge), lambda s, n, *_: (s, n, 0)),
            whole(weights),
        ]
        + [whole(a) for a in par],
        out_specs=[
            row_spec,
            row_spec,
            pl.BlockSpec((1, 4, HALO, edge, chans), lambda s, n, *_: (s, 0, 0, 0, 0)),
            pl.BlockSpec((units, chans), lambda s, n, *_: (0, 0)),
            pl.BlockSpec((units, chans), lambda s, n, *_: (0, 0)),
            pl.BlockSpec((units, 128), lambda s, n, *_: (0, 0)),
            pl.BlockSpec((5, 8, chans), lambda s, n, *_: (0, 0, 0)),
        ],
        scratch_shapes=[
            pltpu.VMEM((STEP_ROWS, edge, chans), F32),
            pltpu.VMEM((edge * edge, chans), F32),
            pltpu.VMEM((chans, units), BF16),
            pltpu.VMEM((chans, units), BF16),
            pltpu.VMEM((units, 128), F32),
        ]
        + margin_scratch(slots, edge, chans),
    )
    cells = slots * edge * edge
    return pl.pallas_call(
        mlp_kernel,
        grid_spec=grid_spec,
        out_shape=[
            jax.ShapeDtypeStruct(state.shape, BF16),
            jax.ShapeDtypeStruct(state.shape, BF16),
            jax.ShapeDtypeStruct((slots, 4, HALO, edge, chans), BF16),
            jax.ShapeDtypeStruct((units, chans), F32),
            jax.ShapeDtypeStruct((units, chans), F32),
            jax.ShapeDtypeStruct((units, 128), F32),
            jax.ShapeDtypeStruct((5, 8, chans), F32),
        ],
        compiler_params=params(VMEM_MIB),
        cost_estimate=pl.CostEstimate(
            flops=12 * cells * units * chans, bytes_accessed=14 * cells * chans, transcendentals=0
        ),
        name="mlp",
    )(table, me, *sources, conv, state, cot, mask, weights, *par)


def tap_grad_kernel(table_ref, me_ref, *refs):
    sources = refs[:5]
    state_ref, mask_ref, grad_ref = refs[5:8]
    late, out_ref = refs[8:12], refs[12]
    padded, totals, small, grad_s = refs[13:17]
    gup, gdown, upacc, vec = refs[17:21]
    late_sem, window, sem = refs[21:]
    tile, tiles = pl.program_id(0), pl.num_programs(0)
    block, blocks = pl.program_id(1), pl.num_programs(1)
    height, edge, chans = grad_s.shape

    def late_copies():
        return [
            pltpu.make_async_copy(source, target, late_sem.at[k])
            for k, (source, target) in enumerate(zip(late, (gup, gdown, upacc, vec)))
        ]

    @pl.when((tile == 0) & (block == 0))
    def _():
        start_window(sources, window, sem)
        for copy in late_copies():
            copy.start()
        totals[...] = jnp.zeros_like(totals)
        zero_margins(padded)

    @pl.when(block == 0)
    def _():
        fill_masked(padded, state_ref, mask_ref)

    @pl.when((tile == 0) & (block == 0))
    def _():
        wait_window(sources, window, sem)

    @pl.when(block == 0)
    def _():
        fill_margins(padded, window, table_ref, me_ref, tile)

    grad_s[...] = grad_ref[0].astype(F32)
    for b in range(KSIZE):

        def body(n, sums, b=b):
            sums = list(sums)
            for g in range(edge // 8):
                grads = [grad_s[n * CONV_ROWS + i, g * 8 : g * 8 + 8] for i in range(CONV_ROWS)]
                for r in range(CONV_ROWS + KSIZE - 1):
                    row = block * height + n * CONV_ROWS + r
                    cells = padded[row, pl.ds(g * 8 + b, 8), :]
                    for a in range(KSIZE):
                        if 0 <= r - a < CONV_ROWS:
                            sums[a] = sums[a] + cells * grads[r - a]
            return tuple(sums)

        start = tuple(totals[a * KSIZE + b] for a in range(KSIZE))
        sums = lax.fori_loop(0, height // CONV_ROWS, body, start)
        for a in range(KSIZE):
            totals[a * KSIZE + b] = sums[a]

    @pl.when((tile == tiles - 1) & (block == blocks - 1))
    def _():
        for copy in late_copies():
            copy.wait()
        small[...] = jnp.zeros_like(small)
        small[0:TAPS] = jnp.sum(totals[...], 1)
        small[TAPS : TAPS + 5] = jnp.sum(vec[...], 1)
        units = upacc.shape[0]
        for u in range(units // 128):
            small[TAPS + 5 + u : TAPS + 6 + u] = jnp.sum(
                upacc[u * 128 : (u + 1) * 128].T, 0, keepdims=True
            )
        high = small[...].astype(BF16)
        rest = (small[...] - high.astype(F32)).astype(BF16)
        count, rows = out_ref.shape[0], small.shape[0]
        share = units // count
        for d in range(count):
            part = slice(d * share, (d + 1) * share)
            out_ref[d, 0:share] = gup[part].astype(BF16)
            out_ref[d, share : 2 * share] = gdown[part].astype(BF16)
            out_ref[d, 2 * share : 2 * share + rows] = high
            out_ref[d, 2 * share + rows :] = rest


def tap_grad_call(table, me, sources, state, mask, grad, gup, gdown, upacc, vec, count):
    slots, edge, _, chans = state.shape
    rows = TAPS + 5 + upacc.shape[0] // 128
    rows = -(-rows // 16) * 16
    length = 2 * (upacc.shape[0] // count) + 2 * rows
    grid_spec = pltpu.PrefetchScalarGridSpec(
        num_scalar_prefetch=2,
        grid=(slots, edge // TAP_ROWS),
        in_specs=[pl.BlockSpec(memory_space=pl.ANY)] * 5
        + [
            pl.BlockSpec((1, edge, edge, chans), lambda s, n, *_: (s, 0, 0, 0)),
            pl.BlockSpec((1, edge, edge), lambda s, n, *_: (s, 0, 0)),
            pl.BlockSpec((1, TAP_ROWS, edge, chans), lambda s, n, *_: (s, n, 0, 0)),
        ]
        + [pl.BlockSpec(memory_space=pl.ANY)] * 4,
        out_specs=pl.BlockSpec((count, length, chans), lambda s, n, *_: (0, 0, 0)),
        scratch_shapes=[
            pltpu.VMEM(padded_shape(edge, chans), F32),
            pltpu.VMEM((TAPS, 8, chans), F32),
            pltpu.VMEM((rows, chans), F32),
            pltpu.VMEM((TAP_ROWS, edge, chans), F32),
            pltpu.VMEM(gup.shape, F32),
            pltpu.VMEM(gdown.shape, F32),
            pltpu.VMEM(upacc.shape, F32),
            pltpu.VMEM(vec.shape, F32),
            pltpu.SemaphoreType.DMA((4,)),
        ]
        + window_scratch(slots, edge, chans),
    )
    return pl.pallas_call(
        tap_grad_kernel,
        grid_spec=grid_spec,
        out_shape=jax.ShapeDtypeStruct((count, length, chans), BF16),
        compiler_params=params(VMEM_MIB),
        cost_estimate=conv_cost(slots, edge, chans),
        name="tap_grad",
    )(table, me, *sources, state, mask, grad, gup, gdown, upacc, vec)


def state_grad_kernel(table_ref, me_ref, *refs):
    sources = refs[:5]
    grad_ref, cot_ref, mask_ref, weight_ref, out_ref, padded, conv_s, window, sem = refs[5:]
    tile, block = pl.program_id(0), pl.program_id(1)
    edge, chans = grad_ref.shape[1], grad_ref.shape[3]

    @pl.when((tile == 0) & (block == 0))
    def _():
        start_window(sources, window, sem)
        zero_margins(padded)

    @pl.when(block == 0)
    def _():
        def fill(n, carry):
            for r in range(8):
                i = n * 8 + r
                padded[HALO + i, HALO : HALO + edge] = grad_ref[0, i].astype(F32)
            return carry

        lax.fori_loop(0, edge // 8, fill, 0)

    @pl.when((tile == 0) & (block == 0))
    def _():
        wait_window(sources, window, sem)

    @pl.when(block == 0)
    def _():
        fill_margins(padded, window, table_ref, me_ref, tile)

    for g in range(edge // 8):

        def write(i, value):
            conv_s[i, g * 8 : g * 8 + 8] = value

        conv_rows(padded, weight_ref, block * CONV_ROWS, g * 8, write, chans, True)
    for k in range(0, CONV_ROWS, 8):
        slabs = spread(mask_ref[0, k : k + 8], chans)
        for r in range(8):
            i = k + r
            out_ref[0, i] = (cot_ref[0, i].astype(F32) + slabs[r] * conv_s[i]).astype(BF16)


def state_grad_call(table, me, sources, grad, cot, mask, weights):
    slots, edge, _, chans = cot.shape
    row_spec = pl.BlockSpec((1, CONV_ROWS, edge, chans), lambda s, n, *_: (s, n, 0, 0))
    grid_spec = pltpu.PrefetchScalarGridSpec(
        num_scalar_prefetch=2,
        grid=(slots, edge // CONV_ROWS),
        in_specs=[pl.BlockSpec(memory_space=pl.ANY)] * 5
        + [
            pl.BlockSpec((1, edge, edge, chans), lambda s, n, *_: (s, 0, 0, 0)),
            row_spec,
            pl.BlockSpec((1, CONV_ROWS, edge), lambda s, n, *_: (s, n, 0)),
            pl.BlockSpec((TAPS, chans), lambda s, n, *_: (0, 0)),
        ],
        out_specs=row_spec,
        scratch_shapes=[
            pltpu.VMEM(padded_shape(edge, chans), F32),
            pltpu.VMEM((CONV_ROWS, edge, chans), F32),
        ]
        + window_scratch(slots, edge, chans),
    )
    return pl.pallas_call(
        state_grad_kernel,
        grid_spec=grid_spec,
        out_shape=jax.ShapeDtypeStruct(cot.shape, BF16),
        compiler_params=params(VMEM_MIB),
        cost_estimate=conv_cost(slots, edge, chans),
        name="state_grad",
    )(table, me, *sources, grad, cot, mask, weights)


def total_kernel(pieces_ref, up_ref, down_ref, taps_ref, vec_ref, bias_ref):
    share = up_ref.shape[0]
    rows = (pieces_ref.shape[1] - 2 * share) // 2
    total = pieces_ref[0].astype(F32)
    for d in range(1, pieces_ref.shape[0]):
        total = total + pieces_ref[d].astype(F32)
    up_ref[...] = total[:share]
    down_ref[...] = total[share : 2 * share]
    small = total[2 * share : 2 * share + rows] + total[2 * share + rows :]
    taps_ref[...] = small[:TAPS]
    vec_ref[...] = small[TAPS : TAPS + 5]
    bias_ref[...] = small[TAPS + 5 : TAPS + 5 + bias_ref.shape[0]]


def total_call(pieces, units):
    count, _, chans = pieces.shape
    share = units // count
    shapes = [(share, chans), (share, chans), (TAPS, chans), (5, chans), (units // chans, chans)]
    return pl.pallas_call(
        total_kernel,
        out_shape=[jax.ShapeDtypeStruct(shape, F32) for shape in shapes],
        compiler_params=params(VMEM_MIB),
        name="total",
    )(pieces)


def pair_pairs():
    return [(i, i ^ 1) for i in range(lax.axis_size("tx"))]


def direct(bands):
    return (
        shifted(bands, "tx", 2),
        lax.ppermute(bands, "tx", pair_pairs()),
        shifted(bands, "tx", -2),
    )


def relayed(below, above):
    odd = lax.axis_index("tx") % 2 == 1
    return lax.ppermute(jnp.where(odd, below, above), "tx", pair_pairs())


def per_device(
    tile_state,
    cotangent,
    neighbours,
    land_mask,
    kernel,
    conv_bias,
    norm_gain,
    norm_bias,
    w_up,
    up_bias,
    w_down,
    down_bias,
    layer_scale,
):
    slots, edge, chans = (tile_state.shape[0], tile_state.shape[1], tile_state.shape[3])
    units = w_up.shape[0]
    count = lax.axis_size("tx")
    mask = land_mask.reshape(slots, edge, edge)
    me = lax.axis_index("tx").astype(jnp.int32)[None]
    par = (
        conv_bias[None],
        norm_gain[None],
        norm_bias[None],
        w_up,
        up_bias[None],
        w_down,
        down_bias[None],
        layer_scale[None],
    )

    bands = bands_call(tile_state, mask)
    below, partner, above = direct(bands)
    conv = own_conv_call(tile_state, mask, kernel)
    below, above, conv = lax.optimization_barrier((below, above, conv))
    window = [below, relayed(below, above), bands, partner, above]
    block_out, grad, grad_bands, gup, gdown, upacc, vec = mlp_call(
        neighbours, me, window, conv, tile_state, cotangent, mask, kernel, par
    )
    below, partner, above = direct(grad_bands)

    pieces = tap_grad_call(
        neighbours, me, window, tile_state, mask, grad, gup, gdown, upacc, vec, count
    )
    pieces, below, above, grad = lax.optimization_barrier((pieces, below, above, grad))
    relay = relayed(below, above)
    pieces, relay, grad = lax.optimization_barrier((pieces, relay, grad))
    grad_window = [below, relay, grad_bands, partner, above]
    pieces = lax.all_to_all(pieces, "tx", 0, 0, tiled=True)
    grad_state = state_grad_call(neighbours, me, grad_window, grad, cotangent, mask, kernel)

    grad_up, grad_down, grad_kernel, grad_vectors, grad_up_bias = total_call(pieces, units)
    grad_up_bias = grad_up_bias.reshape(units)
    return (block_out, grad_state, grad_up, grad_down, grad_kernel, grad_vectors, grad_up_bias)


def solution(mesh):
    tiles = P(("groups", "tx"), None, None, None)
    rows = P(("groups", "tx"), None)
    return jax.shard_map(
        per_device,
        mesh=mesh,
        in_specs=(tiles, tiles, rows, rows) + (P(),) * 9,
        out_specs=(tiles, tiles, rows, rows, P("groups", None), P("groups", None), P("groups")),
        check_vma=False,
    )
```
